512 devices in a mesh: dp: 64 (over z, x), tm: 8 (over y, core).
Axes of the slice: x: 4, y: 4, z: 16, core: 2. Of those that a mesh axis runs over, the one named last changes fastest.
Arguments:
- mel: bfloat16 [64, 2560, 640], P('dp', 'tm'), may hold values from -6 to 6
- cotangent: bfloat16 [64, 2560, 1024], P('dp', 'tm'), may hold values from -6 to 6
- conv_one: bfloat16 [240, 256], replicated, may hold values from -0.375 to 0.375
- conv_two: bfloat16 [768, 256], replicated, may hold values from -0.21875 to 0.21875
- conv_three: bfloat16 [768, 256], replicated, may hold values from -0.21875 to 0.21875
- linear_weight: bfloat16 [256, 1024], replicated, may hold values from -0.375 to 0.375
- ln_gain: float32 [1024], replicated, may hold values from 0.5 to 1.5
- ln_bias: float32 [1024], replicated, may hold values from -3 to 3
- proj: bfloat16 [1024, 2048], P(None, 'tm'), may hold values from -0.1875 to 0.1875
- dw_kernel: bfloat16 [9, 1024], replicated, may hold values from -2 to 2
- blocks: int32 [64], replicated, may hold values from 1 to 64, as said below
Outputs:
- grad_conv_one: bfloat16 [240, 256], replicated
- grad_conv_two: bfloat16 [768, 256], replicated
- grad_conv_three: bfloat16 [768, 256], replicated
- grad_lin: bfloat16 [256, 1024], replicated
- grad_gain: bfloat16 [1024], replicated
- grad_bias: bfloat16 [1024], replicated
- grad_kernel: bfloat16 [9, 1024], replicated
The draws below stay inside these ranges and needn't reach their ends.
Inputs may be any that keep to these rules, and one draw needn't show every extreme that they name: blocks sum to 1366 and the largest is exactly 64.
All inputs are finite; a program needn't handle non-finite values.
Results may differ from the reference program's by a relative error of at most 0.017.
Values may be sent and summed in bfloat16 or wider, within the bound.
A program may use at most 64 MiB of HBM per device.

```python
import jax
import jax.numpy as jnp
from jax import lax

D = 1024
MELS = 80
SUBCH = 256
KERNEL = 9
S_DEV = 320
FOLD = 640
BLK_DEV = 64
BLK = 5
TOTAL_BLKS = 1366
REC_ROWS = 2560
ROWS_ALL = 54640
N_DP = 64
N_TM = 8


def draw_blocks(key, part):
    entries = BLK_DEV
    largest = BLK_DEV
    overall = TOTAL_BLKS
    pick_key, grid_key = jax.random.split(jax.random.fold_in(key, 17))
    planted = jax.random.randint(pick_key, (), 0, entries)
    remaining_items = entries - 1
    spare_units = overall - largest - remaining_items
    grid_cells = jax.random.permutation(grid_key, remaining_items * (largest - 1))
    chosen = grid_cells[:spare_units]
    row_lookup = chosen // (largest - 1)
    surplus_units = jnp.sum((row_lookup[None, :] == jnp.arange(remaining_items)[:, None]).astype(jnp.int32), axis=1)
    regular_rows = 1 + surplus_units
    indices = jnp.arange(entries)
    position = jnp.clip(indices - (indices > planted).astype(jnp.int32), 0, remaining_items - 1)
    values = jnp.where(indices == planted, largest, regular_rows[position])
    return values.astype(jnp.int32)


def shard_levels(rng, shape, cuts, least, high):
    def one(axis_at, parts):
        heights = jax.random.uniform(jax.random.fold_in(jax.random.fold_in(rng, 6), axis_at), (parts,), jnp.float32, least / len(cuts), high / len(cuts))
        return jnp.repeat(jnp.exp(heights), shape[axis_at] // parts).reshape((-1,) + (1,) * (len(shape) - axis_at - 1))

    gain = one(*cuts[0])
    for cut in cuts[1:]:
        gain = gain * one(*cut)
    return gain


def scatter_about(key, dims, width, reach, cuts=(), kind=jnp.bfloat16):
    level = shard_levels(key, dims, cuts, -0.22, 0.18) if cuts else 1.0
    values = jax.random.normal(key, dims, jnp.float32) * width * level
    return jnp.minimum(jnp.maximum(values, -reach), reach).astype(kind)


def setup_inputs(seed: int = 0) -> dict:
    streams_of = jax.random.split(jax.random.key(seed), 12)
    mel = scatter_about(streams_of[0], (N_DP, REC_ROWS, FOLD), 1.0, 6.0, ((0, 64), (1, 8)))
    cotangent = scatter_about(streams_of[1], (N_DP, REC_ROWS, D), 1.0, 6.0, ((0, 64), (1, 8)))
    conv_one = scatter_about(streams_of[2], (3 * MELS, SUBCH), (3 * MELS) ** -0.5, 0.375)
    conv_two = scatter_about(streams_of[3], (3 * SUBCH, SUBCH), (3 * SUBCH) ** -0.5, 0.21875)
    conv_three = scatter_about(streams_of[4], (3 * SUBCH, SUBCH), (3 * SUBCH) ** -0.5, 0.21875)
    linear_weight = scatter_about(streams_of[5], (SUBCH, D), SUBCH ** -0.5, 0.375)
    ln_gain = jnp.clip(1.0 + 0.1 * jax.random.normal(streams_of[6], (D,), jnp.float32), 0.5, 1.5)
    ln_bias = scatter_about(streams_of[7], (D,), 0.5, 3.0, (), jnp.float32)
    proj = scatter_about(streams_of[8], (D, 2 * D), D ** -0.5, 0.1875, ((1, 8),))
    dw_kernel = scatter_about(streams_of[9], (KERNEL, D), KERNEL ** -0.5, 2.0)
    blocks = draw_blocks(jax.random.fold_in(streams_of[11], 71), 0)
    return dict(mel=mel, cotangent=cotangent, conv_one=conv_one, conv_two=conv_two, conv_three=conv_three, linear_weight=linear_weight, ln_gain=ln_gain, ln_bias=ln_bias, proj=proj, dw_kernel=dw_kernel, blocks=blocks)


EPSILON = 1e-05

def product(lhs, rhs):
    return jnp.dot(lhs, rhs, preferred_element_type=jnp.float32)

def product_tn(lhs, rhs):
    return lax.dot_general(lhs, rhs, (((0,), (0,)), ((), ())), preferred_element_type=jnp.float32)

def product_nt(lhs, rhs):
    return lax.dot_general(lhs, rhs, (((1,), (1,)), ((), ())), preferred_element_type=jnp.float32)

def make_patches(values, starts):
    last_slot = values[:, -1, :]
    earlier = jnp.concatenate([jnp.zeros_like(last_slot[:1]), last_slot[:-1]], axis=0)
    earlier = earlier * (1 - starts).astype(values.dtype)[:, None]
    before_taps = jnp.concatenate([earlier[:, None, :], values[:, 1:-1:2, :]], axis=1)
    return jnp.concatenate([before_taps, values[:, 0::2, :], values[:, 1::2, :]], axis=2)

def silu_slope(pre_act):
    sigmoid_val = jax.nn.sigmoid(pre_act)
    return sigmoid_val * (1.0 + pre_act * (1.0 - sigmoid_val))

def subsample_forward(mel_rows, starts, conv_one, conv_two, conv_three, linear_weight):
    row_count = mel_rows.shape[0]
    current = mel_rows.reshape(row_count, 8, -1)
    stored = []
    for weight in (conv_one, conv_two, conv_three):
        patches = make_patches(current, starts)
        pre_act = product(patches.reshape(row_count * patches.shape[1], -1), weight)
        stored.append((patches, pre_act))
        current = jax.nn.silu(pre_act).astype(jnp.bfloat16).reshape(row_count, patches.shape[1], -1)
    top_section = current.reshape(row_count, -1)
    hidden = product(top_section, linear_weight).astype(jnp.bfloat16)
    return (hidden, top_section, stored)

def subsample_backward(grad_hidden, top_section, stored, starts, weights, linear_weight):
    row_count = top_section.shape[0]
    grad_lin = product_tn(top_section, grad_hidden)
    grad_act = product_nt(grad_hidden, linear_weight)
    conv_grads = [None, None, None]
    for section_index in (2, 1, 0):
        patches, pre_act = stored[section_index]
        grad_pre = (grad_act.reshape(pre_act.shape) * silu_slope(pre_act)).astype(jnp.bfloat16)
        conv_grads[section_index] = product_tn(patches.reshape(pre_act.shape[0], -1), grad_pre)
        if section_index > 0:
            grad_patch = product_nt(grad_pre, weights[section_index]).reshape(patches.shape)
            input_shape = (row_count, patches.shape[1] * 2, patches.shape[2] // 3)
            _, pullback = jax.vjp(lambda inner: make_patches(inner, starts), jnp.zeros(input_shape, jnp.float32))
            grad_act = pullback(grad_patch)[0]
    return (grad_lin, conv_grads)

def gated_forward(hidden, ln_gain, ln_bias, proj):
    values = hidden.astype(jnp.float32)
    centre = lax.optimization_barrier(jnp.mean(values, axis=-1, keepdims=True))
    spread = lax.optimization_barrier(jnp.mean(jnp.square(values - centre), axis=-1, keepdims=True))
    inverse_std = lax.rsqrt(spread + EPSILON)
    normed = (values - centre) * inverse_std
    shifted = (normed * ln_gain + ln_bias).astype(jnp.bfloat16)
    projected = product(shifted, proj)
    model_width = proj.shape[0]
    linear_part = projected[:, :model_width]
    sigmoid_gate = jax.nn.sigmoid(projected[:, model_width:])
    gated_rows = (linear_part * sigmoid_gate).astype(jnp.bfloat16)
    return (gated_rows, (normed, inverse_std, linear_part, sigmoid_gate))

def gated_backward(grad_gated, state, ln_gain, proj):
    normed, inverse_std, linear_part, sigmoid_gate = state
    upstream = grad_gated.astype(jnp.float32)
    grad_linear = upstream * sigmoid_gate
    grad_gate = upstream * linear_part * sigmoid_gate * (1.0 - sigmoid_gate)
    grad_projected = jnp.concatenate([grad_linear, grad_gate], axis=-1).astype(jnp.bfloat16)
    grad_shifted = product_nt(grad_projected, proj)
    grad_gain = lax.optimization_barrier(jnp.sum(grad_shifted * normed, axis=0))
    grad_bias = lax.optimization_barrier(jnp.sum(grad_shifted, axis=0))
    grad_normed = grad_shifted * ln_gain
    grad_values = inverse_std * (grad_normed - lax.optimization_barrier(jnp.mean(grad_normed, axis=-1, keepdims=True)) - normed * lax.optimization_barrier(jnp.mean(grad_normed * normed, axis=-1, keepdims=True)))
    return (grad_values.astype(jnp.bfloat16), grad_gain, grad_bias)

def reference(mel, cotangent, conv_one, conv_two, conv_three, linear_weight, ln_gain, ln_bias, proj, dw_kernel, blocks):
    share_rows = blocks * BLK
    record_len = share_rows * N_TM
    record_end = jnp.cumsum(record_len)
    record_start = record_end - record_len
    places = jnp.arange(ROWS_ALL, dtype=jnp.int32)
    record_of = lax.optimization_barrier(jnp.sum((record_end[None, :] <= places[:, None]).astype(jnp.int32), axis=1))
    within = places - record_start[record_of]
    row_share = share_rows[record_of]
    share_index = within // row_share
    local_row = within - share_index * row_share
    flat_row = share_index * S_DEV + local_row
    mel_rows = mel[record_of, flat_row]
    cot_rows = cotangent[record_of, flat_row]
    starts = (within == 0).astype(jnp.int32)
    hidden, top_section, stored = subsample_forward(mel_rows, starts, conv_one, conv_two, conv_three, linear_weight)
    gated_rows, state = gated_forward(hidden, ln_gain, ln_bias, proj)
    loss_scale = lax.rsqrt(jnp.float32(ROWS_ALL))
    grad_out = cot_rows.astype(jnp.float32) * loss_scale
    length_row = record_len[record_of]
    half_width = KERNEL // 2
    padded = jnp.pad(gated_rows.astype(jnp.float32), ((half_width, half_width), (0, 0)))
    grad_pad = jnp.zeros_like(padded)
    kernel_terms = []
    for tap_index in range(KERNEL):
        target = within + tap_index - half_width
        inside = ((target >= 0) & (target < length_row)).astype(jnp.float32)[:, None]
        weighted = grad_out * inside
        kernel_terms.append(lax.optimization_barrier(jnp.sum(weighted * padded[tap_index:tap_index + ROWS_ALL], axis=0)))
        grad_pad = grad_pad.at[tap_index:tap_index + ROWS_ALL].add(weighted * dw_kernel[tap_index].astype(jnp.float32))
    grad_gated = grad_pad[half_width:half_width + ROWS_ALL].astype(jnp.bfloat16)
    grad_hidden, grad_gain, grad_bias = gated_backward(grad_gated, state, ln_gain, proj)
    grad_lin, conv_grads = subsample_backward(grad_hidden, top_section, stored, starts, (conv_one, conv_two, conv_three), linear_weight)
    grad_kernel = jnp.stack(kernel_terms, axis=0)
    return (conv_grads[0].astype(jnp.bfloat16), conv_grads[1].astype(jnp.bfloat16), conv_grads[2].astype(jnp.bfloat16), grad_lin.astype(jnp.bfloat16), grad_gain.astype(jnp.bfloat16), grad_bias.astype(jnp.bfloat16), grad_kernel.astype(jnp.bfloat16))
```

```python
import jax
import jax.numpy as jnp
from jax import lax
from jax.sharding import PartitionSpec as P

EPSILON = 1e-05
BF = jnp.bfloat16
F32 = jnp.float32


def mm(lhs, rhs):
    return jnp.dot(lhs, rhs, preferred_element_type=F32)


def mm_tn(lhs, rhs):
    return lax.dot_general(lhs, rhs, (((0,), (0,)), ((), ())), preferred_element_type=F32)


def mm_nt(lhs, rhs):
    return lax.dot_general(lhs, rhs, (((1,), (1,)), ((), ())), preferred_element_type=F32)


def roll(values, shift):
    return jnp.roll(values, shift, axis=0)


def silu(z):
    return (z * jax.nn.sigmoid(z)).astype(BF)


def through_silu(grad, z):
    s = jax.nn.sigmoid(z)
    return (grad * (s * (1.0 + z * (1.0 - s)))).astype(BF)


def wide_conv_one(conv):
    bins = conv.shape[0] // 3
    columns = []
    for slot in range(4):
        if slot == 0:
            column = jnp.concatenate(
                [conv[bins:], jnp.zeros((6 * bins, conv.shape[1]), conv.dtype), conv[:bins]], axis=0
            )
        else:
            top = (2 * slot - 1) * bins
            column = jnp.pad(conv, ((top, 9 * bins - top - 3 * bins), (0, 0)))
        columns.append(column)
    return jnp.concatenate(columns, axis=1)


def narrow_conv_one(wide):
    bins = wide.shape[0] // 9
    ch = wide.shape[1] // 4
    total = jnp.concatenate([wide[8 * bins :, :ch], wide[: 2 * bins, :ch]], axis=0)
    for slot in range(1, 4):
        top = (2 * slot - 1) * bins
        total = total + wide[top : top + 3 * bins, slot * ch : (slot + 1) * ch]
    return total


def per_device(
    mel,
    cotangent,
    conv_one,
    conv_two,
    conv_three,
    linear_weight,
    ln_gain,
    ln_bias,
    proj,
    dw_kernel,
    blocks,
):
    tm_count = lax.axis_size("tm")
    tm_rank = lax.axis_index("tm")
    dp_count = lax.axis_size("dp")
    rows_dev = mel.shape[1]
    bins = conv_one.shape[0] // 3
    ch = conv_two.shape[1]
    width = linear_weight.shape[1]
    taps = dw_kernel.shape[0]
    half = taps // 2
    rows = rows_dev + 16
    total_blocks = (dp_count * dp_count + 2) // 3
    block_rows = rows_dev // dp_count
    live = blocks[lax.axis_index("dp")] * block_rows
    scale = lax.rsqrt(F32(total_blocks * block_rows * tm_count))

    proj_full = lax.all_gather(proj, "tm", axis=1, tiled=True)
    up = [(i, i + 1) for i in range(tm_count - 1)]
    down = [(i + 1, i) for i in range(tm_count - 1)]
    tail = lax.dynamic_slice_in_dim(mel[0], live - half - 1, half + 1, 0)
    before = lax.ppermute(tail, "tm", up)
    after = lax.ppermute(mel[0, :half], "tm", down)
    ids = jnp.arange(rows, dtype=jnp.int32)[:, None]
    own = ids < live
    x = jnp.where(own, jnp.pad(mel[0], ((0, rows - rows_dev), (0, 0))), jnp.zeros((), BF))
    x = lax.dynamic_update_slice(x, after, (live, 0))
    x = lax.dynamic_update_slice(x, before, (rows - half - 1, 0))
    valid = (
        own
        | ((ids < live + half) & (tm_rank < tm_count - 1))
        | ((ids >= rows - half) & (tm_rank > 0))
    )
    cot = jnp.where(own, jnp.pad(cotangent[0], ((0, rows - rows_dev), (0, 0))), jnp.zeros((), BF))

    x_wide = jnp.concatenate([x, roll(x[:, 7 * bins :], 1)], axis=1)
    w_one = wide_conv_one(conv_one)
    z1 = mm(x_wide, w_one)
    a1 = silu(z1)
    z2 = jnp.concatenate(
        [
            mm(a1[:, : 2 * ch], conv_two[ch:]) + mm(roll(a1[:, 3 * ch :], 1), conv_two[:ch]),
            mm(a1[:, ch:], conv_two),
        ],
        axis=1,
    )
    a2 = silu(z2)
    z3 = mm(a2, conv_three[ch:]) + mm(roll(a2[:, ch:], 1), conv_three[:ch])
    a3 = silu(z3)
    h = mm(a3, linear_weight).astype(BF).astype(F32)
    centred = h - jnp.mean(h, axis=-1, keepdims=True)
    inverse = lax.rsqrt(jnp.mean(jnp.square(centred), axis=-1, keepdims=True) + EPSILON)
    n = centred * inverse
    u = (n * ln_gain + ln_bias).astype(BF)
    m = mm(u, proj_full)
    value = m[:, :width]
    gate = jax.nn.sigmoid(m[:, width:])
    gated = jnp.where(valid, (value * gate).astype(BF).astype(F32), 0.0)

    c = cot.astype(F32) * scale
    kernel_float = dw_kernel.astype(F32)
    grad_kernel = []
    eg = jnp.zeros((rows, width), F32)
    for k in range(taps):
        grad_kernel.append(jnp.sum(c * roll(gated, half - k), axis=0))
        eg = eg + roll(c, k - half) * kernel_float[k]
    grad_kernel = jnp.stack(grad_kernel, axis=0)
    eg = jnp.where(valid, eg, 0.0).astype(BF).astype(F32)

    value_grad = eg * gate
    gate_grad = value_grad * value * (1.0 - gate)
    em = jnp.concatenate([value_grad, gate_grad], axis=1).astype(BF)
    du = mm_nt(em, proj_full)
    grad_gain = jnp.sum(du * n, axis=0)
    grad_bias = jnp.sum(du, axis=0)
    e = du * ln_gain
    dh = (
        inverse
        * (e - jnp.mean(e, axis=-1, keepdims=True) - n * jnp.mean(e * n, axis=-1, keepdims=True))
    ).astype(BF)
    grad_lin = mm_tn(a3, dh)
    ez3 = through_silu(mm_nt(dh, linear_weight), z3)
    ez3_next = roll(ez3, -1)
    grad_three = jnp.concatenate([mm_tn(a2[:, ch:], ez3_next), mm_tn(a2, ez3)], axis=0)
    da2 = mm_nt(ez3, conv_three[ch:])
    da2 = jnp.concatenate([da2[:, :ch], da2[:, ch:] + mm_nt(ez3_next, conv_three[:ch])], axis=1)
    ez2 = through_silu(da2, z2)
    first, second = ez2[:, :ch], ez2[:, ch:]
    first_next = roll(first, -1)
    grad_two = (
        jnp.concatenate([mm_tn(a1[:, 3 * ch :], first_next), mm_tn(a1[:, : 2 * ch], first)], axis=0)
        + mm_tn(a1[:, ch:], second)
    )
    left = mm_nt(first, conv_two[ch:])
    right = mm_nt(second, conv_two)
    over = mm_nt(first_next, conv_two[:ch])
    da1 = jnp.concatenate(
        [left[:, :ch], left[:, ch:] + right[:, :ch], right[:, ch : 2 * ch], right[:, 2 * ch :] + over],
        axis=1,
    )
    ez1 = through_silu(da1, z1)
    grad_one = narrow_conv_one(mm_tn(x_wide, ez1))
    summed = lax.psum(
        (grad_one, grad_two, grad_three, grad_lin, grad_gain, grad_bias, grad_kernel), ("dp", "tm")
    )
    return tuple(piece.astype(BF) for piece in summed)


def solution(mesh):
    return jax.shard_map(
        per_device,
        mesh=mesh,
        in_specs=(
            P("dp", "tm", None),
            P("dp", "tm", None),
            P(),
            P(),
            P(),
            P(),
            P(),
            P(),
            P(None, "tm"),
            P(),
            P(),
        ),
        out_specs=(P(), P(), P(), P(), P(), P(), P()),
        check_vma=False,
    )
```

```python
import functools

import jax
import jax.numpy as jnp
from jax import lax
from jax.experimental import pallas as pl
from jax.experimental.pallas import tpu as pltpu
from jax.sharding import PartitionSpec as P

EPSILON = 1e-05
BF = jnp.bfloat16
F32 = jnp.float32


def mm(lhs, rhs):
    return jnp.dot(lhs, rhs, preferred_element_type=F32)


def mm_tn(lhs, rhs):
    return lax.dot_general(lhs, rhs, (((0,), (0,)), ((), ())), preferred_element_type=F32)


def mm_nt(lhs, rhs):
    return lax.dot_general(lhs, rhs, (((1,), (1,)), ((), ())), preferred_element_type=F32)


def roll(values, shift):
    return jnp.roll(values, shift, axis=0)


def silu(z):
    return (z * jax.nn.sigmoid(z)).astype(BF)


def through_silu(grad, z):
    s = jax.nn.sigmoid(z)
    return (grad * (s * (1.0 + z * (1.0 - s)))).astype(BF)


def wide_conv_one(conv):
    bins = conv.shape[0] // 3
    columns = []
    for slot in range(4):
        if slot == 0:
            column = jnp.concatenate(
                [conv[bins:], jnp.zeros((6 * bins, conv.shape[1]), conv.dtype), conv[:bins]], axis=0
            )
        else:
            top = (2 * slot - 1) * bins
            column = jnp.pad(conv, ((top, 9 * bins - top - 3 * bins), (0, 0)))
        columns.append(column)
    return jnp.concatenate(columns, axis=1)


def narrow_conv_one(wide):
    bins = wide.shape[0] // 9
    ch = wide.shape[1] // 4
    total = jnp.concatenate([wide[8 * bins :, :ch], wide[: 2 * bins, :ch]], axis=0)
    for slot in range(1, 4):
        top = (2 * slot - 1) * bins
        total = total + wide[top : top + 3 * bins, slot * ch : (slot + 1) * ch]
    return total


NX = 4
CORES = 2
PIECE = 96
LANES = 256
SUB = 8


def row_loop(count, step, body):
    lax.fori_loop(0, count // step, lambda i, carry: (body(pl.multiple_of(i * step, step)), carry)[1], 0)


def sum_kernel(
    nz, ny, one, two, three, lin, small, o_one, o_two, o_three, o_lin, o_small,
    acc, out, snd, from_core, from_y, from_x, z_acc, z_snd, from_z, z_out, send_sem, recv_sem,
):
    dp, tm = lax.axis_index("dp"), lax.axis_index("tm")
    z, x = dp // NX, dp % NX
    y, core = tm // CORES, tm % CORES
    chunk = NX * PIECE
    half = ny * chunk

    def at_core():
        return (dp, y * CORES + (1 - core))

    def at_y(d):
        return (dp, ((y + d) % ny) * CORES + core)

    def at_x(d):
        return (z * NX + (x + d) % NX, tm)

    def at_z(d):
        return (((z + d) % nz) * NX + x, tm)

    barrier = pltpu.get_barrier_semaphore()
    peers = [at_z(d) for d in range(1, nz)] + [at_x(d) for d in range(1, NX)]
    peers = peers + [at_y(d) for d in range(1, ny)] + [at_core()]
    for peer in peers:
        pl.semaphore_signal(barrier, inc=1, device_id=peer, device_id_type=pl.DeviceIdType.MESH)

    first = 0
    places = []
    for src, dst in ((one, o_one), (two, o_two), (three, o_three), (lin, o_lin), (small, o_small)):
        for lane in range(0, src.shape[1], LANES):
            places.append((src, dst, lane, first, src.shape[0]))
            first += src.shape[0]
    for src, _, lane, top, count in places:
        step = 16 if count % 48 else 48

        def fill(i, src=src, lane=lane, top=top, step=step):
            acc[pl.ds(top + i, step), :] = src[pl.ds(i, step), pl.ds(lane, LANES)]

        row_loop(count, step, fill)
    rest = acc.shape[0] - first
    acc[pl.ds(first, rest), :] = jnp.zeros((rest, LANES), F32)

    started = []

    def send(src, dst, peer):
        k = len(started)
        copy = pltpu.make_async_remote_copy(
            src_ref=src,
            dst_ref=dst,
            send_sem=send_sem.at[k],
            recv_sem=recv_sem.at[k],
            device_id=peer,
            device_id_type=pl.DeviceIdType.MESH,
        )
        copy.start()
        started.append(copy)
        return copy

    mine = core * half
    theirs = (1 - core) * half
    order = list(range(1, ny)) + [0]
    pl.semaphore_wait(barrier, len(peers))
    core_copies = []
    for d in order:
        place = pl.multiple_of(((y + d) % ny) * chunk, PIECE)

        def narrow(i, place=place):
            at = pl.multiple_of(theirs + place + i, 48)
            snd[pl.ds(at, 48), :] = acc[pl.ds(at, 48), :].astype(BF)

        row_loop(chunk, 48, narrow)
        core_copies.append(
            send(
                snd.at[pl.ds(pl.multiple_of(theirs + place, PIECE), chunk)],
                from_core.at[pl.ds(place, chunk)],
                at_core(),
            )
        )
    y_copies = []
    for d, copy in zip(order, core_copies):
        copy.wait_recv()
        place = pl.multiple_of(((y + d) % ny) * chunk, PIECE)

        def add_core(i, place=place, d=d):
            at = pl.multiple_of(mine + place + i, 48)
            total = acc[pl.ds(at, 48), :] + from_core[
                pl.ds(pl.multiple_of(place + i, 48), 48), :
            ].astype(F32)
            if d == 0:
                acc[pl.ds(at, 48), :] = total
            else:
                snd[pl.ds(at, 48), :] = total.astype(BF)

        row_loop(chunk, 48, add_core)
        if d:
            y_copies.append(
                send(
                    snd.at[pl.ds(pl.multiple_of(mine + place, PIECE), chunk)],
                    from_y.at[d - 1],
                    at_y(d),
                )
            )
    for copy in y_copies:
        copy.wait_recv()
    own = pl.multiple_of(mine + y * chunk, PIECE)

    def add_y(i):
        at = pl.multiple_of(own + i, 48)
        total = acc[pl.ds(at, 48), :]
        for d in range(1, ny):
            total = total + from_y[d - 1, pl.ds(i, 48), :].astype(F32)
        acc[pl.ds(at, 48), :] = total
        snd[pl.ds(at, 48), :] = total.astype(BF)

    row_loop(chunk, 48, add_y)
    x_copies = []
    for d in range(1, NX):
        place = pl.multiple_of(own + ((x + d) % NX) * PIECE, PIECE)
        x_copies.append(send(snd.at[pl.ds(place, PIECE)], from_x.at[d - 1], at_x(d)))
    for copy in x_copies:
        copy.wait_recv()
    piece = pl.multiple_of(own + x * PIECE, PIECE)
    total = acc[pl.ds(piece, PIECE), :]
    for d in range(1, NX):
        total = total + from_x[d - 1].astype(F32)
    parts = PIECE // SUB
    total = total.reshape(parts, SUB, LANES)
    z_acc[pl.ds(0, parts)] = total
    z_snd[pl.ds(0, parts)] = total.astype(BF)
    z_acc[pl.ds(parts, nz - parts)] = jnp.zeros((nz - parts, SUB, LANES), F32)
    z_snd[pl.ds(parts, nz - parts)] = jnp.zeros((nz - parts, SUB, LANES), BF)
    far = sorted(range(1, nz), key=lambda d: -min(d, nz - d))
    z_copies = [send(z_snd.at[(z + d) % nz], from_z.at[d - 1], at_z(d)) for d in far]
    for copy in z_copies:
        copy.wait_recv()
    total = z_acc[z]
    for d in range(1, nz):
        total = total + from_z[d - 1].astype(F32)
    z_out[z] = total.astype(BF)
    z_copies = [send(z_out.at[z], z_out.at[z], at_z(d)) for d in far]
    for copy in z_copies:
        copy.wait_recv()
    done = z_out[pl.ds(0, parts)].astype(F32).reshape(PIECE, LANES)
    out[pl.ds(piece, PIECE), :] = done.astype(BF)
    whole = out.at[pl.ds(piece, PIECE)]
    x_copies = [send(whole, whole, at_x(d)) for d in range(1, NX)]
    for copy in x_copies:
        copy.wait_recv()
    whole = out.at[pl.ds(own, chunk)]
    y_copies = [send(whole, whole, at_y(d)) for d in range(1, ny)]
    core_copies = [send(whole, whole, at_core())]
    for d, copy in zip(range(1, ny), y_copies):
        copy.wait_recv()
        place = pl.multiple_of(mine + ((y - d + ny) % ny) * chunk, PIECE)
        whole = out.at[pl.ds(place, chunk)]
        core_copies.append(send(whole, whole, at_core()))
    for copy in core_copies:
        copy.wait_recv()
    for copy in started:
        copy.wait_send()
    for _, dst, lane, top, count in places:
        step = 16 if count % 48 else 48

        def drain(i, dst=dst, lane=lane, top=top, step=step):
            dst[pl.ds(i, step), pl.ds(lane, LANES)] = out[pl.ds(top + i, step), :]

        row_loop(count, step, drain)


def sum_everywhere(pieces, nz, ny):
    total = CORES * ny * NX * PIECE
    copies = 2 * (ny + (ny - 1) + (NX - 1) + (nz - 1))
    vmem = pl.BlockSpec(memory_space=pltpu.VMEM)
    return pl.pallas_call(
        functools.partial(sum_kernel, nz, ny),
        out_shape=[jax.ShapeDtypeStruct(p.shape, BF) for p in pieces],
        in_specs=[vmem] * len(pieces),
        out_specs=[vmem] * len(pieces),
        scratch_shapes=[
            pltpu.VMEM((total, LANES), F32),
            pltpu.VMEM((total, LANES), BF),
            pltpu.VMEM((total, LANES), BF),
            pltpu.VMEM((total // CORES, LANES), BF),
            pltpu.VMEM((ny - 1, NX * PIECE, LANES), BF),
            pltpu.VMEM((NX - 1, PIECE, LANES), BF),
            pltpu.VMEM((nz, SUB, LANES), F32),
            pltpu.VMEM((nz, SUB, LANES), BF),
            pltpu.VMEM((nz - 1, SUB, LANES), BF),
            pltpu.VMEM((nz, SUB, LANES), BF),
            pltpu.SemaphoreType.DMA((copies,)),
            pltpu.SemaphoreType.DMA((copies,)),
        ],
        compiler_params=pltpu.CompilerParams(collective_id=0, has_side_effects=True),
    )(*pieces)


def per_device(
    mel,
    cotangent,
    conv_one,
    conv_two,
    conv_three,
    linear_weight,
    ln_gain,
    ln_bias,
    proj,
    dw_kernel,
    blocks,
):
    tm_count = lax.axis_size("tm")
    tm_rank = lax.axis_index("tm")
    dp_count = lax.axis_size("dp")
    rows_dev = mel.shape[1]
    bins = conv_one.shape[0] // 3
    ch = conv_two.shape[1]
    width = linear_weight.shape[1]
    taps = dw_kernel.shape[0]
    half = taps // 2
    rows = rows_dev + 16
    total_blocks = (dp_count * dp_count + 2) // 3
    block_rows = rows_dev // dp_count
    live = blocks[lax.axis_index("dp")] * block_rows
    scale = lax.rsqrt(F32(total_blocks * block_rows * tm_count))

    proj_full = lax.all_gather(proj, "tm", axis=1, tiled=True)
    up = [(i, i + 1) for i in range(tm_count - 1)]
    down = [(i + 1, i) for i in range(tm_count - 1)]
    tail = lax.dynamic_slice_in_dim(mel[0], live - half - 1, half + 1, 0)
    before = lax.ppermute(tail, "tm", up)
    after = lax.ppermute(mel[0, :half], "tm", down)
    ids = jnp.arange(rows, dtype=jnp.int32)[:, None]
    own = ids < live
    x = jnp.where(own, jnp.pad(mel[0], ((0, rows - rows_dev), (0, 0))), jnp.zeros((), BF))
    x = lax.dynamic_update_slice(x, after, (live, 0))
    x = lax.dynamic_update_slice(x, before, (rows - half - 1, 0))
    valid = (
        own
        | ((ids < live + half) & (tm_rank < tm_count - 1))
        | ((ids >= rows - half) & (tm_rank > 0))
    )
    cot = jnp.where(own, jnp.pad(cotangent[0], ((0, rows - rows_dev), (0, 0))), jnp.zeros((), BF))

    x_wide = jnp.concatenate([x, roll(x[:, 7 * bins :], 1)], axis=1)
    w_one = wide_conv_one(conv_one)
    z1 = mm(x_wide, w_one)
    a1 = silu(z1)
    z2 = jnp.concatenate(
        [
            mm(a1[:, : 2 * ch], conv_two[ch:]) + mm(roll(a1[:, 3 * ch :], 1), conv_two[:ch]),
            mm(a1[:, ch:], conv_two),
        ],
        axis=1,
    )
    a2 = silu(z2)
    z3 = mm(a2, conv_three[ch:]) + mm(roll(a2[:, ch:], 1), conv_three[:ch])
    a3 = silu(z3)
    h = mm(a3, linear_weight).astype(BF).astype(F32)
    centred = h - jnp.mean(h, axis=-1, keepdims=True)
    inverse = lax.rsqrt(jnp.mean(jnp.square(centred), axis=-1, keepdims=True) + EPSILON)
    n = centred * inverse
    u = (n * ln_gain + ln_bias).astype(BF)
    m = mm(u, proj_full)
    value = m[:, :width]
    gate = jax.nn.sigmoid(m[:, width:])
    gated = jnp.where(valid, (value * gate).astype(BF).astype(F32), 0.0)

    c = cot.astype(F32) * scale
    kernel_float = dw_kernel.astype(F32)
    grad_kernel = []
    eg = jnp.zeros((rows, width), F32)
    for k in range(taps):
        grad_kernel.append(jnp.sum(c * roll(gated, half - k), axis=0))
        eg = eg + roll(c, k - half) * kernel_float[k]
    grad_kernel = jnp.stack(grad_kernel, axis=0)
    eg = jnp.where(valid, eg, 0.0).astype(BF).astype(F32)

    value_grad = eg * gate
    gate_grad = value_grad * value * (1.0 - gate)
    em = jnp.concatenate([value_grad, gate_grad], axis=1).astype(BF)
    du = mm_nt(em, proj_full)
    grad_gain = jnp.sum(du * n, axis=0)
    grad_bias = jnp.sum(du, axis=0)
    e = du * ln_gain
    dh = (
        inverse
        * (e - jnp.mean(e, axis=-1, keepdims=True) - n * jnp.mean(e * n, axis=-1, keepdims=True))
    ).astype(BF)
    grad_lin = mm_tn(a3, dh)
    ez3 = through_silu(mm_nt(dh, linear_weight), z3)
    ez3_next = roll(ez3, -1)
    grad_three = jnp.concatenate([mm_tn(a2[:, ch:], ez3_next), mm_tn(a2, ez3)], axis=0)
    da2 = mm_nt(ez3, conv_three[ch:])
    da2 = jnp.concatenate([da2[:, :ch], da2[:, ch:] + mm_nt(ez3_next, conv_three[:ch])], axis=1)
    ez2 = through_silu(da2, z2)
    first, second = ez2[:, :ch], ez2[:, ch:]
    first_next = roll(first, -1)
    grad_two = (
        jnp.concatenate([mm_tn(a1[:, 3 * ch :], first_next), mm_tn(a1[:, : 2 * ch], first)], axis=0)
        + mm_tn(a1[:, ch:], second)
    )
    left = mm_nt(first, conv_two[ch:])
    right = mm_nt(second, conv_two)
    over = mm_nt(first_next, conv_two[:ch])
    da1 = jnp.concatenate(
        [left[:, :ch], left[:, ch:] + right[:, :ch], right[:, ch : 2 * ch], right[:, 2 * ch :] + over],
        axis=1,
    )
    ez1 = through_silu(da1, z1)
    grad_one = narrow_conv_one(mm_tn(x_wide, ez1))
    small = jnp.concatenate(
        [grad_kernel, grad_gain[None], grad_bias[None], jnp.zeros((16 - taps - 2, width), F32)], axis=0
    )
    one, two, three, lin, small = sum_everywhere(
        (grad_one, grad_two, grad_three, grad_lin, small), dp_count // NX, tm_count // CORES
    )
    return (one, two, three, lin, small[taps], small[taps + 1], small[:taps])


def solution(mesh):
    return jax.shard_map(
        per_device,
        mesh=mesh,
        in_specs=(
            P("dp", "tm", None),
            P("dp", "tm", None),
            P(),
            P(),
            P(),
            P(),
            P(),
            P(),
            P(None, "tm"),
            P(),
            P(),
        ),
        out_specs=(P(), P(), P(), P(), P(), P(), P()),
        check_vma=False,
    )
```

```python
import functools

import jax
import jax.numpy as jnp
from jax import lax
from jax.experimental import pallas as pl
from jax.experimental.pallas import tpu as pltpu
from jax.sharding import PartitionSpec as P

EPSILON = 1e-05
BF = jnp.bfloat16
F32 = jnp.float32


def mm(lhs, rhs):
    return jnp.dot(lhs, rhs, preferred_element_type=F32)


def mm_tn(lhs, rhs):
    return lax.dot_general(lhs, rhs, (((0,), (0,)), ((), ())), preferred_element_type=F32)


def mm_nt(lhs, rhs):
    return lax.dot_general(lhs, rhs, (((1,), (1,)), ((), ())), preferred_element_type=F32)


def silu(z):
    return (z * jax.nn.sigmoid(z)).astype(BF)


def through_silu(grad, z):
    s = jax.nn.sigmoid(z)
    return (grad * (s * (1.0 + z * (1.0 - s)))).astype(BF)


def wide_conv_one(conv):
    bins, ch = conv.shape[0] // 3, conv.shape[1]
    rows = 768

    def zeros(count):
        return jnp.zeros((count, ch), conv.dtype)

    columns = [jnp.concatenate([conv[bins:], zeros(rows - 3 * bins), conv[:bins]], axis=0)]
    for slot in range(1, 4):
        top = (2 * slot - 1) * bins
        columns.append(jnp.pad(conv, ((top, rows - top - 3 * bins), (0, 0))))
    return jnp.concatenate(columns, axis=1)


NX = 4
CORES = 2
PIECE = 96
LANES = 256
SUB = 8


def row_loop(count, step, body):
    lax.fori_loop(0, count // step, lambda i, carry: (body(pl.multiple_of(i * step, step)), carry)[1], 0)


def sum_kernel(
    nz, ny, one, two, three, lin, small, o_one, o_two, o_three, o_lin, o_small,
    acc, out, snd, from_core, from_y, from_x, z_acc, z_snd, from_z, z_out, send_sem, recv_sem,
):
    dp, tm = lax.axis_index("dp"), lax.axis_index("tm")
    z, x = dp // NX, dp % NX
    y, core = tm // CORES, tm % CORES
    chunk = NX * PIECE
    half = ny * chunk

    def at_core():
        return (dp, y * CORES + (1 - core))

    def at_y(d):
        return (dp, ((y + d) % ny) * CORES + core)

    def at_x(d):
        return (z * NX + (x + d) % NX, tm)

    def at_z(d):
        return (((z + d) % nz) * NX + x, tm)

    barrier = pltpu.get_barrier_semaphore()
    peers = [at_z(d) for d in range(1, nz)] + [at_x(d) for d in range(1, NX)]
    peers = peers + [at_y(d) for d in range(1, ny)] + [at_core()]
    for peer in peers:
        pl.semaphore_signal(barrier, inc=1, device_id=peer, device_id_type=pl.DeviceIdType.MESH)

    first = 0
    places = []
    for src, dst in ((one, o_one), (two, o_two), (three, o_three), (lin, o_lin), (small, o_small)):
        for lane in range(0, src.shape[1], LANES):
            places.append((src, dst, lane, first, src.shape[0]))
            first += src.shape[0]
    for src, _, lane, top, count in places:
        step = 16 if count % 48 else 48

        def fill(i, src=src, lane=lane, top=top, step=step):
            acc[pl.ds(top + i, step), :] = src[pl.ds(i, step), pl.ds(lane, LANES)]

        row_loop(count, step, fill)
    rest = acc.shape[0] - first
    acc[pl.ds(first, rest), :] = jnp.zeros((rest, LANES), F32)

    started = []

    def send(src, dst, peer):
        k = len(started)
        copy = pltpu.make_async_remote_copy(
            src_ref=src,
            dst_ref=dst,
            send_sem=send_sem.at[k],
            recv_sem=recv_sem.at[k],
            device_id=peer,
            device_id_type=pl.DeviceIdType.MESH,
        )
        copy.start()
        started.append(copy)
        return copy

    mine = core * half
    theirs = (1 - core) * half
    order = list(range(1, ny)) + [0]
    pl.semaphore_wait(barrier, len(peers))
    core_copies = []
    for d in order:
        place = pl.multiple_of(((y + d) % ny) * chunk, PIECE)

        def narrow(i, place=place):
            at = pl.multiple_of(theirs + place + i, 48)
            snd[pl.ds(at, 48), :] = acc[pl.ds(at, 48), :].astype(BF)

        row_loop(chunk, 48, narrow)
        core_copies.append(
            send(
                snd.at[pl.ds(pl.multiple_of(theirs + place, PIECE), chunk)],
                from_core.at[pl.ds(place, chunk)],
                at_core(),
            )
        )
    y_copies = []
    for d, copy in zip(order, core_copies):
        copy.wait_recv()
        place = pl.multiple_of(((y + d) % ny) * chunk, PIECE)

        def add_core(i, place=place, d=d):
            at = pl.multiple_of(mine + place + i, 48)
            total = acc[pl.ds(at, 48), :] + from_core[
                pl.ds(pl.multiple_of(place + i, 48), 48), :
            ].astype(F32)
            if d == 0:
                acc[pl.ds(at, 48), :] = total
            else:
                snd[pl.ds(at, 48), :] = total.astype(BF)

        row_loop(chunk, 48, add_core)
        if d:
            y_copies.append(
                send(
                    snd.at[pl.ds(pl.multiple_of(mine + place, PIECE), chunk)],
                    from_y.at[d - 1],
                    at_y(d),
                )
            )
    for copy in y_copies:
        copy.wait_recv()
    own = pl.multiple_of(mine + y * chunk, PIECE)

    def add_y(i):
        at = pl.multiple_of(own + i, 48)
        total = acc[pl.ds(at, 48), :]
        for d in range(1, ny):
            total = total + from_y[d - 1, pl.ds(i, 48), :].astype(F32)
        acc[pl.ds(at, 48), :] = total
        snd[pl.ds(at, 48), :] = total.astype(BF)

    row_loop(chunk, 48, add_y)
    x_copies = []
    for d in range(1, NX):
        place = pl.multiple_of(own + ((x + d) % NX) * PIECE, PIECE)
        x_copies.append(send(snd.at[pl.ds(place, PIECE)], from_x.at[d - 1], at_x(d)))
    for copy in x_copies:
        copy.wait_recv()
    piece = pl.multiple_of(own + x * PIECE, PIECE)
    total = acc[pl.ds(piece, PIECE), :]
    for d in range(1, NX):
        total = total + from_x[d - 1].astype(F32)
    parts = PIECE // SUB
    total = total.reshape(parts, SUB, LANES)
    z_acc[pl.ds(0, parts)] = total
    z_snd[pl.ds(0, parts)] = total.astype(BF)
    z_acc[pl.ds(parts, nz - parts)] = jnp.zeros((nz - parts, SUB, LANES), F32)
    z_snd[pl.ds(parts, nz - parts)] = jnp.zeros((nz - parts, SUB, LANES), BF)
    far = sorted(range(1, nz), key=lambda d: -min(d, nz - d))
    z_copies = [send(z_snd.at[(z + d) % nz], from_z.at[d - 1], at_z(d)) for d in far]
    for copy in z_copies:
        copy.wait_recv()
    total = z_acc[z]
    for d in range(1, nz):
        total = total + from_z[d - 1].astype(F32)
    z_out[z] = total.astype(BF)
    z_copies = [send(z_out.at[z], z_out.at[z], at_z(d)) for d in far]
    for copy in z_copies:
        copy.wait_recv()
    done = z_out[pl.ds(0, parts)].astype(F32).reshape(PIECE, LANES)
    out[pl.ds(piece, PIECE), :] = done.astype(BF)
    whole = out.at[pl.ds(piece, PIECE)]
    x_copies = [send(whole, whole, at_x(d)) for d in range(1, NX)]
    for copy in x_copies:
        copy.wait_recv()
    whole = out.at[pl.ds(own, chunk)]
    y_copies = [send(whole, whole, at_y(d)) for d in range(1, ny)]
    core_copies = [send(whole, whole, at_core())]
    for d, copy in zip(range(1, ny), y_copies):
        copy.wait_recv()
        place = pl.multiple_of(mine + ((y - d + ny) % ny) * chunk, PIECE)
        whole = out.at[pl.ds(place, chunk)]
        core_copies.append(send(whole, whole, at_core()))
    for copy in core_copies:
        copy.wait_recv()
    for copy in started:
        copy.wait_send()
    for _, dst, lane, top, count in places:
        step = 16 if count % 48 else 48

        def drain(i, dst=dst, lane=lane, top=top, step=step):
            dst[pl.ds(i, step), pl.ds(lane, LANES)] = out[pl.ds(top + i, step), :]

        row_loop(count, step, drain)


def sum_everywhere(pieces, nz, ny):
    total = CORES * ny * NX * PIECE
    copies = 2 * (ny + (ny - 1) + (NX - 1) + (nz - 1))
    vmem = pl.BlockSpec(memory_space=pltpu.VMEM)
    return pl.pallas_call(
        functools.partial(sum_kernel, nz, ny),
        out_shape=[jax.ShapeDtypeStruct(p.shape, BF) for p in pieces],
        in_specs=[vmem] * len(pieces),
        out_specs=[vmem] * len(pieces),
        scratch_shapes=[
            pltpu.VMEM((total, LANES), F32),
            pltpu.VMEM((total, LANES), BF),
            pltpu.VMEM((total, LANES), BF),
            pltpu.VMEM((total // CORES, LANES), BF),
            pltpu.VMEM((ny - 1, NX * PIECE, LANES), BF),
            pltpu.VMEM((NX - 1, PIECE, LANES), BF),
            pltpu.VMEM((nz, SUB, LANES), F32),
            pltpu.VMEM((nz, SUB, LANES), BF),
            pltpu.VMEM((nz - 1, SUB, LANES), BF),
            pltpu.VMEM((nz, SUB, LANES), BF),
            pltpu.SemaphoreType.DMA((copies,)),
            pltpu.SemaphoreType.DMA((copies,)),
        ],
        compiler_params=pltpu.CompilerParams(collective_id=0, has_side_effects=True),
    )(*pieces)


ROWS = 336
STEP = 48
RIM = 16


def work_kernel(
    tm_n, half, scale, live_ref, mel, cot, proj, w_one, w_two, w_three, lin, gain, bias, taps,
    one, two, three, g_lin, small,
    full, xw, up_snd, up_rcv, down_rcv, z1, z2, z3, a1, a2, a3, n_ref, inv_ref, u_ref, du_ref,
    eg_ref, gated_ref, em, dh_ref, sums, own_sem, send_sem, recv_sem,
):
    dp, tm = lax.axis_index("dp"), lax.axis_index("tm")
    ny = tm_n // CORES
    y, core = tm // CORES, tm % CORES
    own_rows = mel.shape[0]
    width = lin.shape[1]
    live = live_ref[0]

    def at(d):
        return (dp, (tm + d) % tm_n)

    barrier = pltpu.get_barrier_semaphore()
    for d in range(1, tm_n):
        pl.semaphore_signal(barrier, inc=1, device_id=at(d), device_id_type=pl.DeviceIdType.MESH)

    first_row = lax.broadcasted_iota(jnp.int32, (RIM, own_rows), 0)
    column = lax.broadcasted_iota(jnp.int32, (RIM, own_rows), 1)
    pick = (column - live == first_row - RIM) & (first_row >= RIM - half - 1)
    up_snd[...] = mm(pick.astype(F32).astype(BF), mel[...]).astype(BF)
    pl.semaphore_wait(barrier, tm_n - 1)

    started = []

    def send(src, dst, peer):
        k = len(started)
        copy = pltpu.make_async_remote_copy(
            src_ref=src,
            dst_ref=dst,
            send_sem=send_sem.at[k],
            recv_sem=recv_sem.at[k],
            device_id=peer,
            device_id_type=pl.DeviceIdType.MESH,
        )
        copy.start()
        started.append(copy)
        return copy

    partner = (dp, y * CORES + (1 - core))
    up = send(up_snd, up_rcv, at(1))
    down = send(mel.at[pl.ds(0, RIM)], down_rcv, at(tm_n - 1))
    y_copies = [(d, send(proj, full.at[tm], (dp, ((y + d) % ny) * CORES + core))) for d in (1, 3, 2)]
    core_copies = [send(proj, full.at[tm], partner)]
    keep = pltpu.make_async_copy(proj, full.at[tm], own_sem)
    keep.start()

    def mask(count, lanes):
        ids = lax.broadcasted_iota(jnp.int32, (count, lanes), 0)
        right = (ids < live + half) & (tm < tm_n - 1)
        left = (ids >= ROWS - half) & (tm > 0)
        return (ids < live) | right | left

    def cot_block(cols):
        c = cot[:, cols].astype(F32) * scale
        ids = lax.broadcasted_iota(jnp.int32, c.shape, 0)
        c = jnp.where(ids < live, c, 0.0)
        return jnp.concatenate([c, jnp.zeros((ROWS - own_rows, c.shape[1]), F32)], axis=0)

    def back_taps(i, carry):
        cols = pl.ds(pl.multiple_of(i * 128, 128), 128)
        c = cot_block(cols)
        total = jnp.zeros_like(c)
        for k in range(2 * half + 1):
            shifted = pltpu.roll(c, (k - half) % ROWS, 0) if k != half else c
            total = total + shifted * taps[k : k + 1, cols]
        eg_ref[:, cols] = jnp.where(mask(ROWS, 128), total, 0.0).astype(BF)
        return carry

    lax.fori_loop(0, width // 128, back_taps, 0)

    up.wait_recv()
    down.wait_recv()

    def place(i, carry):
        at_row = pl.multiple_of(i * 64, 64)
        rows = lax.broadcasted_iota(jnp.int32, (64, RIM), 0) + at_row
        slot = lax.broadcasted_iota(jnp.int32, (64, RIM), 1)
        pick = (rows - live == slot) & (slot < half) & (tm < tm_n - 1)
        ids = lax.broadcasted_iota(jnp.int32, (64, mel.shape[1]), 0) + at_row
        value = jnp.where(ids < live, mel[pl.ds(at_row, 64), :].astype(F32), 0.0)
        value = value + mm(pick.astype(F32).astype(BF), down_rcv[...])
        xw[pl.ds(at_row, 64), 0:640] = value.astype(BF)
        return carry

    lax.fori_loop(0, own_rows // 64, place, 0)
    rows = lax.broadcasted_iota(jnp.int32, (RIM, RIM), 0) + own_rows
    slot = lax.broadcasted_iota(jnp.int32, (RIM, RIM), 1)
    pick = (rows - live == slot) & (slot < half) & (tm < tm_n - 1)
    value = mm(pick.astype(F32).astype(BF), down_rcv[...])
    value = value + jnp.where(tm > 0, 1.0, 0.0) * up_rcv[...].astype(F32)
    xw[own_rows:ROWS, 0:640] = value.astype(BF)
    xw[:, 640:768] = pltpu.roll(xw[:, 512:640].astype(F32), 1, 0).astype(BF)

    windows = ((0, 256), (0, 384), (128, 512), (384, 640))
    for j, (low, high) in enumerate(windows):
        cols = slice(256 * j, 256 * j + 256)
        z = mm(xw[:, low:high], w_one[low:high, cols])
        if j == 0:
            z = z + mm(xw[:, 640:768], w_one[640:768, cols])
        z1[:, cols] = z
        a1[:, cols] = silu(z)
    z = mm(a1[:, :512], w_two[256:, :]) + pltpu.roll(mm(a1[:, 768:], w_two[:256, :]), 1, 0)
    z2[:, :256] = z
    a2[:, :256] = silu(z)
    z = mm(a1[:, 256:], w_two[...])
    z2[:, 256:] = z
    a2[:, 256:] = silu(z)
    z = mm(a2[...], w_three[256:, :]) + pltpu.roll(mm(a2[:, 256:], w_three[:256, :]), 1, 0)
    z3[...] = z
    a3[...] = silu(z)

    def project(i, carry):
        cols = pl.ds(pl.multiple_of(i * 256, 256), 256)
        n_ref[:, cols] = mm(a3[...], lin[:, cols]).astype(BF).astype(F32)
        return carry

    lax.fori_loop(0, width // 256, project, 0)

    def normalise(i, carry):
        rows = pl.ds(pl.multiple_of(i * STEP, STEP), STEP)
        h = n_ref[rows, :]
        h = h - jnp.mean(h, axis=-1, keepdims=True)
        inverse = lax.rsqrt(jnp.mean(h * h, axis=-1, keepdims=True) + EPSILON)
        n = h * inverse
        n_ref[rows, :] = n
        inv_ref[rows, :] = jnp.broadcast_to(inverse, (STEP, 128))
        u_ref[rows, :] = (n * gain[...] + bias[...]).astype(BF)
        return carry

    lax.fori_loop(0, ROWS // STEP, normalise, 0)

    for d, copy in y_copies:
        copy.wait_recv()
        came = ((y - d + ny) % ny) * CORES + core
        core_copies.append(send(full.at[came], full.at[came], partner))
    keep.wait()
    for copy in core_copies:
        copy.wait_recv()

    def gates(i, carry):
        cols = pl.ds(pl.multiple_of(i * 256, 256), 256)
        value = mm(u_ref[...], full[i])
        gate = jax.nn.sigmoid(mm(u_ref[...], full[i + ny]))
        gated = (value * gate).astype(BF).astype(F32)
        gated_ref[:, cols] = jnp.where(mask(ROWS, 256), gated, 0.0)
        grad = eg_ref[:, cols].astype(F32) * gate
        em[i] = grad.astype(BF)
        em[i + ny] = (grad * value * (1.0 - gate)).astype(BF)
        return carry

    lax.fori_loop(0, width // 256, gates, 0)

    def tap_grads(i, carry):
        cols = pl.ds(pl.multiple_of(i * 128, 128), 128)
        c = cot_block(cols)
        gated = gated_ref[:, cols]
        sums_k = []
        for k in range(2 * half + 1):
            shifted = pltpu.roll(c, (k - half) % ROWS, 0) if k != half else c
            sums_k.append(jnp.sum(gated * shifted, axis=0, keepdims=True))
        sums_k.append(jnp.zeros((16 - len(sums_k), 128), F32))
        small[:, cols] = jnp.concatenate(sums_k, axis=0)
        return carry

    lax.fori_loop(0, width // 128, tap_grads, 0)

    def unproject(i, carry):
        cols = pl.multiple_of(i * 256, 256)
        total = mm_nt(em[0], full[0, pl.ds(cols, 256), :])
        for t in range(1, tm_n):
            total = total + mm_nt(em[t], full[t, pl.ds(cols, 256), :])
        du_ref[:, pl.ds(cols, 256)] = total
        return carry

    lax.fori_loop(0, width // 256, unproject, 0)
    sums[...] = jnp.zeros_like(sums)

    def denormalise(i, carry):
        rows = pl.ds(pl.multiple_of(i * STEP, STEP), STEP)
        du = du_ref[rows, :]
        n = n_ref[rows, :]
        sums[0:1, :] += jnp.sum(du * n, axis=0, keepdims=True)
        sums[1:2, :] += jnp.sum(du, axis=0, keepdims=True)
        e = du * gain[...]
        e_mean = jnp.mean(e, axis=-1, keepdims=True)
        en_mean = jnp.mean(e * n, axis=-1, keepdims=True)
        dh_ref[rows, :] = (inv_ref[rows, 0:1] * (e - e_mean - n * en_mean)).astype(BF)
        return carry

    lax.fori_loop(0, ROWS // STEP, denormalise, 0)
    small[2 * half + 1 : 2 * half + 3, :] = sums[0:2, :]

    def lin_grad(i, carry):
        cols = pl.ds(pl.multiple_of(i * 256, 256), 256)
        g_lin[:, cols] = mm_tn(a3[...], dh_ref[:, cols])
        return carry

    lax.fori_loop(0, width // 256, lin_grad, 0)

    def later(v):
        return pltpu.roll(v.astype(F32), ROWS - 1, 0)

    ez3 = through_silu(mm_nt(dh_ref[...], lin[...]), z3[...])
    three[256:, :] = mm_tn(a2[...], ez3)
    three[:256, :] = mm_tn(a2[:, 256:], later(ez3).astype(BF))
    first = through_silu(mm_nt(ez3, w_three[256:512, :]), z2[:, :256])
    over = later(mm_nt(ez3, w_three[:256, :]))
    second = through_silu(mm_nt(ez3, w_three[512:, :]) + over, z2[:, 256:])
    side = mm_tn(a1[:, 256:], second)
    two[:256, :] = mm_tn(a1[:, 768:], later(first).astype(BF)) + side[:256]
    two[256:, :] = mm_tn(a1[:, :512], first) + side[256:]
    da = (
        mm_nt(first, w_two[256:512, :]),
        mm_nt(first, w_two[512:, :]) + mm_nt(second, w_two[:256, :]),
        mm_nt(second, w_two[256:512, :]),
        mm_nt(second, w_two[512:, :]) + later(mm_nt(first, w_two[:256, :])),
    )
    tops = (0, 80, 112, 16)
    total = None
    for j in (1, 2, 3):
        low, high = windows[j]
        ez = through_silu(da[j], z1[:, 256 * j : 256 * j + 256])
        term = mm_tn(xw[:, low:high], ez)[tops[j] : tops[j] + 240]
        total = term if total is None else total + term
    ez = through_silu(da[0], z1[:, :256])
    here = mm_tn(xw[:, :256], ez)[:160]
    gone = mm_tn(xw[:, 640:768], ez)[48:]
    one[...] = total + jnp.concatenate([gone, here], axis=0)
    for copy in started:
        copy.wait_send()


def work(live, mel, cot, proj, w_one, w_two, w_three, lin, gain, bias, taps, tm_n, half, scale):
    width = lin.shape[1]
    vmem = pl.BlockSpec(memory_space=pltpu.VMEM)
    ny = tm_n // CORES
    copies = 2 + 2 * (ny - 1) + 1

    def buf(*shape, dtype=BF):
        return pltpu.VMEM(shape, dtype)

    return pl.pallas_call(
        functools.partial(work_kernel, tm_n, half, scale),
        out_shape=[
            jax.ShapeDtypeStruct(shape, F32)
            for shape in ((240, 256), (768, 256), (768, 256), (256, width), (16, width))
        ],
        in_specs=[pl.BlockSpec(memory_space=pltpu.SMEM)] + [vmem] * 10,
        out_specs=[vmem] * 5,
        scratch_shapes=[
            buf(tm_n, *proj.shape),
            buf(ROWS, 768),
            buf(RIM, 640),
            buf(RIM, 640),
            buf(RIM, 640),
            buf(ROWS, 1024, dtype=F32),
            buf(ROWS, 512, dtype=F32),
            buf(ROWS, 256, dtype=F32),
            buf(ROWS, 1024),
            buf(ROWS, 512),
            buf(ROWS, 256),
            buf(ROWS, width, dtype=F32),
            buf(ROWS, 128, dtype=F32),
            buf(ROWS, width),
            buf(ROWS, width, dtype=F32),
            buf(ROWS, width),
            buf(ROWS, width, dtype=F32),
            buf(tm_n, ROWS, 256),
            buf(ROWS, width),
            buf(8, width, dtype=F32),
            pltpu.SemaphoreType.DMA,
            pltpu.SemaphoreType.DMA((copies,)),
            pltpu.SemaphoreType.DMA((copies,)),
        ],
        compiler_params=pltpu.CompilerParams(
            collective_id=1, has_side_effects=True, vmem_limit_bytes=56 * 1024 * 1024
        ),
    )(live, mel, cot, proj, w_one, w_two, w_three, lin, gain, bias, taps)


def per_device(
    mel,
    cotangent,
    conv_one,
    conv_two,
    conv_three,
    linear_weight,
    ln_gain,
    ln_bias,
    proj,
    dw_kernel,
    blocks,
):
    tm_count = lax.axis_size("tm")
    dp_count = lax.axis_size("dp")
    block_rows = mel.shape[1] // dp_count
    taps = dw_kernel.shape[0]
    total_rows = (dp_count * dp_count + 2) // 3 * block_rows * tm_count
    live = (blocks[lax.axis_index("dp")] * block_rows)[None]
    results = work(
        live,
        mel[0],
        cotangent[0],
        proj,
        wide_conv_one(conv_one),
        conv_two,
        conv_three,
        linear_weight,
        ln_gain[None],
        ln_bias[None],
        jnp.pad(dw_kernel.astype(F32), ((0, 16 - taps), (0, 0))),
        tm_count,
        taps // 2,
        total_rows**-0.5,
    )
    one, two, three, lin, small = sum_everywhere(results, dp_count // NX, tm_count // CORES)
    return (one, two, three, lin, small[taps], small[taps + 1], small[:taps])


def solution(mesh):
    return jax.shard_map(
        per_device,
        mesh=mesh,
        in_specs=(
            P("dp", "tm", None),
            P("dp", "tm", None),
            P(),
            P(),
            P(),
            P(),
            P(),
            P(),
            P(None, "tm"),
            P(),
            P(),
        ),
        out_specs=(P(), P(), P(), P(), P(), P(), P()),
        check_vma=False,
    )
```

```python
import functools

import jax
import jax.numpy as jnp
from jax import lax
from jax.experimental import pallas as pl
from jax.experimental.pallas import tpu as pltpu
from jax.sharding import PartitionSpec as P

EPSILON = 1e-05
BF = jnp.bfloat16
F32 = jnp.float32


def mm(lhs, rhs):
    return jnp.dot(lhs, rhs, preferred_element_type=F32)


def mm_tn(lhs, rhs):
    return lax.dot_general(lhs, rhs, (((0,), (0,)), ((), ())), preferred_element_type=F32)


def mm_nt(lhs, rhs):
    return lax.dot_general(lhs, rhs, (((1,), (1,)), ((), ())), preferred_element_type=F32)


def silu(z):
    return (z * jax.nn.sigmoid(z)).astype(BF)


def through_silu(grad, z):
    s = jax.nn.sigmoid(z)
    return (grad * (s * (1.0 + z * (1.0 - s)))).astype(BF)


NX = 4
CORES = 2
PIECE = 48
LANES = 256
SUB = 8


def row_loop(count, step, body):
    lax.fori_loop(0, count // step, lambda i, carry: (body(pl.multiple_of(i * step, step)), carry)[1], 0)


def sum_kernel(
    nz, ny, one, two, three, lin, small, result,
    acc, out, snd, from_core, from_first, from_second, z_acc, z_snd, from_z, z_out,
    send_sem, recv_sem,
):
    dp, tm = lax.axis_index("dp"), lax.axis_index("tm")
    z, x = dp // NX, dp % NX
    y, core = tm // CORES, tm % CORES
    fan = NX
    chunk = fan * PIECE
    half = fan * chunk

    def at_y(d):
        return (dp, ((y + d) % ny) * CORES + core)

    def at_x(d):
        return (z * NX + (x + d) % NX, tm)

    def at_z(d):
        return (((z + d) % nz) * NX + x, tm)

    at_core = (dp, y * CORES + (1 - core))
    colours = ((0, y, at_y, x, at_x), (1, x, at_x, y, at_y))

    barrier = pltpu.get_barrier_semaphore()
    peers = [at_z(d) for d in range(1, nz)] + [at_x(d) for d in range(1, NX)]
    peers = peers + [at_y(d) for d in range(1, ny)] + [at_core]
    for peer in peers:
        pl.semaphore_signal(barrier, inc=1, device_id=peer, device_id_type=pl.DeviceIdType.MESH)

    top = 0
    for src in (one, two, three, lin, small):
        for lane in range(0, src.shape[1], LANES):
            step = 16 if src.shape[0] % 48 else 48

            def fill(i, src=src, lane=lane, top=top, step=step):
                acc[pl.ds(top + i, step), :] = src[pl.ds(i, step), pl.ds(lane, LANES)]

            row_loop(src.shape[0], step, fill)
            top += src.shape[0]
    rest = acc.shape[0] - top
    acc[pl.ds(top, rest), :] = jnp.zeros((rest, LANES), F32)

    started = []

    def send(src, dst, peer):
        k = len(started)
        copy = pltpu.make_async_remote_copy(
            src_ref=src,
            dst_ref=dst,
            send_sem=send_sem.at[k],
            recv_sem=recv_sem.at[k],
            device_id=peer,
            device_id_type=pl.DeviceIdType.MESH,
        )
        copy.start()
        started.append(copy)
        return copy

    def mine(colour):
        return (colour * CORES + core) * half

    def theirs(colour):
        return (colour * CORES + 1 - core) * half

    order = list(range(1, fan)) + [0]
    pl.semaphore_wait(barrier, len(peers))
    core_copies = []
    for d in order:
        for colour, first, _, _, _ in colours:
            place = ((first + d) % fan) * chunk

            def narrow(i, place=place, colour=colour):
                at = pl.multiple_of(theirs(colour) + place + i, PIECE)
                snd[pl.ds(at, PIECE), :] = acc[pl.ds(at, PIECE), :].astype(BF)

            row_loop(chunk, PIECE, narrow)
            core_copies.append(
                send(
                    snd.at[pl.ds(pl.multiple_of(theirs(colour) + place, PIECE), chunk)],
                    from_core.at[pl.ds(pl.multiple_of(colour * half + place, PIECE), chunk)],
                    at_core,
                )
            )
    first_copies = []
    for d in order:
        for colour, first, at_first, _, _ in colours:
            core_copies.pop(0).wait_recv()
            place = ((first + d) % fan) * chunk

            def add_core(i, place=place, d=d, colour=colour):
                at = pl.multiple_of(mine(colour) + place + i, PIECE)
                came = from_core[pl.ds(pl.multiple_of(colour * half + place + i, PIECE), PIECE), :]
                total = acc[pl.ds(at, PIECE), :] + came.astype(F32)
                if d == 0:
                    acc[pl.ds(at, PIECE), :] = total
                else:
                    snd[pl.ds(at, PIECE), :] = total.astype(BF)

            row_loop(chunk, PIECE, add_core)
            if d:
                at = pl.multiple_of(mine(colour) + place, PIECE)
                first_copies.append(
                    send(snd.at[pl.ds(at, chunk)], from_first.at[colour, d - 1], at_first(d))
                )
    for copy in first_copies:
        copy.wait_recv()
    second_copies = []
    for colour, first, _, second, at_second in colours:
        own = mine(colour) + first * chunk

        def add_first(i, own=own, colour=colour):
            at = pl.multiple_of(own + i, PIECE)
            total = acc[pl.ds(at, PIECE), :]
            for d in range(1, fan):
                total = total + from_first[colour, d - 1, pl.ds(i, PIECE), :].astype(F32)
            acc[pl.ds(at, PIECE), :] = total
            snd[pl.ds(at, PIECE), :] = total.astype(BF)

        row_loop(chunk, PIECE, add_first)
        for d in range(1, fan):
            at = pl.multiple_of(own + ((second + d) % fan) * PIECE, PIECE)
            second_copies.append(
                send(snd.at[pl.ds(at, PIECE)], from_second.at[colour, d - 1], at_second(d))
            )
    parts = PIECE // SUB
    for colour, first, _, second, _ in colours:
        for _ in range(1, fan):
            second_copies.pop(0).wait_recv()
        piece = pl.multiple_of(mine(colour) + first * chunk + second * PIECE, PIECE)
        total = acc[pl.ds(piece, PIECE), :]
        for d in range(1, fan):
            total = total + from_second[colour, d - 1].astype(F32)
        total = total.reshape(parts, SUB, LANES)
        z_acc[pl.ds(colour * parts, parts)] = total
        z_snd[pl.ds(colour * parts, parts)] = total.astype(BF)
    used = 2 * parts
    z_acc[pl.ds(used, nz - used)] = jnp.zeros((nz - used, SUB, LANES), F32)
    z_snd[pl.ds(used, nz - used)] = jnp.zeros((nz - used, SUB, LANES), BF)
    far = sorted(range(1, nz), key=lambda d: -min(d, nz - d))
    z_copies = [send(z_snd.at[(z + d) % nz], from_z.at[d - 1], at_z(d)) for d in far]
    for copy in z_copies:
        copy.wait_recv()
    total = z_acc[z]
    for d in range(1, nz):
        total = total + from_z[d - 1].astype(F32)
    z_out[z] = total.astype(BF)
    z_copies = [send(z_out.at[z], z_out.at[z], at_z(d)) for d in far]
    for copy in z_copies:
        copy.wait_recv()
    for colour, first, _, second, at_second in colours:
        done = z_out[pl.ds(colour * parts, parts)].astype(F32).reshape(PIECE, LANES)
        piece = pl.multiple_of(mine(colour) + first * chunk + second * PIECE, PIECE)
        out[pl.ds(piece, PIECE), :] = done.astype(BF)
        whole = out.at[pl.ds(piece, PIECE)]
        second_copies.extend([send(whole, whole, at_second(d)) for d in range(1, fan)])
    for copy in second_copies:
        copy.wait_recv()
    first_copies = []
    for colour, first, at_first, _, _ in colours:
        whole = out.at[pl.ds(pl.multiple_of(mine(colour) + first * chunk, PIECE), chunk)]
        first_copies.append([send(whole, whole, at_first(d)) for d in range(1, fan)])
        core_copies.append(send(whole, whole, at_core))
    for d in range(1, fan):
        for colour, first, _, _, _ in colours:
            first_copies[colour][d - 1].wait_recv()
            place = pl.multiple_of(mine(colour) + ((first - d + fan) % fan) * chunk, PIECE)
            whole = out.at[pl.ds(place, chunk)]
            core_copies.append(send(whole, whole, at_core))
    for copy in core_copies:
        copy.wait_recv()

    def drain(i):
        result[pl.ds(i, PIECE), :] = out[pl.ds(i, PIECE), :]

    row_loop(out.shape[0], PIECE, drain)
    for copy in started:
        copy.wait_send()


def unpack_kernel(packed, one, two, three, lin, small):
    top = 0
    for dst in (one, two, three, lin, small):
        for lane in range(0, dst.shape[1], LANES):
            step = 16 if dst.shape[0] % 48 else 48

            def drain(i, dst=dst, lane=lane, top=top, step=step):
                dst[pl.ds(i, step), pl.ds(lane, LANES)] = packed[pl.ds(top + i, step), :]

            row_loop(dst.shape[0], step, drain)
            top += dst.shape[0]


def sum_everywhere(pieces, nz, ny):
    total = 2 * CORES * NX * NX * PIECE
    copies = 2 * (2 * (NX + 2 * (NX - 1)) + nz - 1)
    vmem = pl.BlockSpec(memory_space=pltpu.VMEM)
    packed = pl.pallas_call(
        functools.partial(sum_kernel, nz, ny),
        out_shape=jax.ShapeDtypeStruct((total, LANES), BF),
        in_specs=[vmem] * len(pieces),
        out_specs=vmem,
        scratch_shapes=[
            pltpu.VMEM((total, LANES), F32),
            pltpu.VMEM((total, LANES), BF),
            pltpu.VMEM((total, LANES), BF),
            pltpu.VMEM((total // CORES, LANES), BF),
            pltpu.VMEM((2, NX - 1, NX * PIECE, LANES), BF),
            pltpu.VMEM((2, NX - 1, PIECE, LANES), BF),
            pltpu.VMEM((nz, SUB, LANES), F32),
            pltpu.VMEM((nz, SUB, LANES), BF),
            pltpu.VMEM((nz - 1, SUB, LANES), BF),
            pltpu.VMEM((nz, SUB, LANES), BF),
            pltpu.SemaphoreType.DMA((copies,)),
            pltpu.SemaphoreType.DMA((copies,)),
        ],
        compiler_params=pltpu.CompilerParams(collective_id=0, has_side_effects=True),
    )(*pieces)
    return pl.pallas_call(
        unpack_kernel,
        out_shape=[jax.ShapeDtypeStruct(p.shape, BF) for p in pieces],
        in_specs=[vmem],
        out_specs=[vmem] * len(pieces),
    )(packed)


ROWS = 336
STEP = 48
RIM = 16


def work_kernel(
    tm_n, half, block_rows, scale, blocks, mel_ref, cot_ref, proj, conv_one, w_two, w_three, lin, gain, bias, taps,
    one, two, three, g_lin, small,
    full, w_one, xw, up_snd, up_rcv, down_rcv, z1, z2, z3, a1, a2, a3, n_ref, inv_ref, u_ref, du_ref,
    eg_ref, gated_ref, em, dh_ref, sums, own_sem, send_sem, recv_sem,
):
    dp, tm = lax.axis_index("dp"), lax.axis_index("tm")
    ny = tm_n // CORES
    y, core = tm // CORES, tm % CORES
    mel, cot = mel_ref.at[0], cot_ref.at[0]
    own_rows = mel.shape[0]
    width = lin.shape[1]
    live = blocks[dp] * block_rows

    def at(d):
        return (dp, (tm + d) % tm_n)

    barrier = pltpu.get_barrier_semaphore()
    for d in range(1, tm_n):
        pl.semaphore_signal(barrier, inc=1, device_id=at(d), device_id_type=pl.DeviceIdType.MESH)

    first_row = lax.broadcasted_iota(jnp.int32, (RIM, own_rows), 0)
    column = lax.broadcasted_iota(jnp.int32, (RIM, own_rows), 1)
    pick = (column - live == first_row - RIM) & (first_row >= RIM - half - 1)
    up_snd[...] = mm(pick.astype(F32).astype(BF), mel[...]).astype(BF)
    bins = conv_one.shape[0] // 3

    def clear(i):
        w_one[pl.ds(i, 48), :] = jnp.zeros((48, 1024), BF)

    row_loop(768, 48, clear)
    w_one[: 2 * bins, :256] = conv_one[bins:, :]
    w_one[768 - bins :, :256] = conv_one[:bins, :]
    for j in range(1, 4):
        above = (2 * j - 1) * bins
        w_one[above : above + 3 * bins, 256 * j : 256 * j + 256] = conv_one[...]
    pl.semaphore_wait(barrier, tm_n - 1)

    started = []

    def send(src, dst, peer):
        k = len(started)
        copy = pltpu.make_async_remote_copy(
            src_ref=src,
            dst_ref=dst,
            send_sem=send_sem.at[k],
            recv_sem=recv_sem.at[k],
            device_id=peer,
            device_id_type=pl.DeviceIdType.MESH,
        )
        copy.start()
        started.append(copy)
        return copy

    partner = (dp, y * CORES + (1 - core))
    up = send(up_snd, up_rcv, at(1))
    down = send(mel.at[pl.ds(0, RIM)], down_rcv, at(tm_n - 1))
    y_copies = [(d, send(proj, full.at[tm], (dp, ((y + d) % ny) * CORES + core))) for d in (1, 3, 2)]
    core_copies = [send(proj, full.at[tm], partner)]
    keep = pltpu.make_async_copy(proj, full.at[tm], own_sem)
    keep.start()

    def mask(count, lanes):
        ids = lax.broadcasted_iota(jnp.int32, (count, lanes), 0)
        right = (ids < live + half) & (tm < tm_n - 1)
        left = (ids >= ROWS - half) & (tm > 0)
        return (ids < live) | right | left

    def cot_block(cols):
        c = cot[:, cols].astype(F32) * scale
        ids = lax.broadcasted_iota(jnp.int32, c.shape, 0)
        c = jnp.where(ids < live, c, 0.0)
        return jnp.concatenate([c, jnp.zeros((ROWS - own_rows, c.shape[1]), F32)], axis=0)

    def back_taps(i, carry):
        cols = pl.ds(pl.multiple_of(i * 128, 128), 128)
        c = cot_block(cols)
        total = jnp.zeros_like(c)
        weights = taps[:, cols].astype(F32)
        for k in range(2 * half + 1):
            shifted = pltpu.roll(c, (k - half) % ROWS, 0) if k != half else c
            total = total + shifted * weights[k : k + 1]
        eg_ref[:, cols] = jnp.where(mask(ROWS, 128), total, 0.0).astype(BF)
        return carry

    lax.fori_loop(0, width // 128, back_taps, 0)

    up.wait_recv()
    down.wait_recv()

    def place(i, carry):
        at_row = pl.multiple_of(i * 64, 64)
        rows = lax.broadcasted_iota(jnp.int32, (64, RIM), 0) + at_row
        slot = lax.broadcasted_iota(jnp.int32, (64, RIM), 1)
        pick = (rows - live == slot) & (slot < half) & (tm < tm_n - 1)
        ids = lax.broadcasted_iota(jnp.int32, (64, mel.shape[1]), 0) + at_row
        value = jnp.where(ids < live, mel[pl.ds(at_row, 64), :].astype(F32), 0.0)
        value = value + mm(pick.astype(F32).astype(BF), down_rcv[...])
        xw[pl.ds(at_row, 64), 0:640] = value.astype(BF)
        return carry

    lax.fori_loop(0, own_rows // 64, place, 0)
    rows = lax.broadcasted_iota(jnp.int32, (RIM, RIM), 0) + own_rows
    slot = lax.broadcasted_iota(jnp.int32, (RIM, RIM), 1)
    pick = (rows - live == slot) & (slot < half) & (tm < tm_n - 1)
    value = mm(pick.astype(F32).astype(BF), down_rcv[...])
    value = value + jnp.where(tm > 0, 1.0, 0.0) * up_rcv[...].astype(F32)
    xw[own_rows:ROWS, 0:640] = value.astype(BF)
    xw[:, 640:768] = pltpu.roll(xw[:, 512:640].astype(F32), 1, 0).astype(BF)

    windows = ((0, 256), (0, 384), (128, 512), (384, 640))
    for j, (low, high) in enumerate(windows):
        cols = slice(256 * j, 256 * j + 256)
        z = mm(xw[:, low:high], w_one[low:high, cols])
        if j == 0:
            z = z + mm(xw[:, 640:768], w_one[640:768, cols])
        z1[:, cols] = z
        a1[:, cols] = silu(z)
    z = mm(a1[:, :512], w_two[256:, :]) + pltpu.roll(mm(a1[:, 768:], w_two[:256, :]), 1, 0)
    z2[:, :256] = z
    a2[:, :256] = silu(z)
    z = mm(a1[:, 256:], w_two[...])
    z2[:, 256:] = z
    a2[:, 256:] = silu(z)
    z = mm(a2[...], w_three[256:, :]) + pltpu.roll(mm(a2[:, 256:], w_three[:256, :]), 1, 0)
    z3[...] = z
    a3[...] = silu(z)

    def project(i, carry):
        cols = pl.ds(pl.multiple_of(i * 256, 256), 256)
        n_ref[:, cols] = mm(a3[...], lin[:, cols]).astype(BF).astype(F32)
        return carry

    lax.fori_loop(0, width // 256, project, 0)

    def normalise(i, carry):
        rows = pl.ds(pl.multiple_of(i * STEP, STEP), STEP)
        h = n_ref[rows, :]
        h = h - jnp.mean(h, axis=-1, keepdims=True)
        inverse = lax.rsqrt(jnp.mean(h * h, axis=-1, keepdims=True) + EPSILON)
        n = h * inverse
        n_ref[rows, :] = n
        inv_ref[rows, :] = jnp.broadcast_to(inverse, (STEP, 128))
        u_ref[rows, :] = (n * gain[...] + bias[...]).astype(BF)
        return carry

    lax.fori_loop(0, ROWS // STEP, normalise, 0)

    for d, copy in y_copies:
        copy.wait_recv()
        came = ((y - d + ny) % ny) * CORES + core
        core_copies.append(send(full.at[came], full.at[came], partner))
    keep.wait()
    for copy in core_copies:
        copy.wait_recv()

    def gates(i, carry):
        cols = pl.ds(pl.multiple_of(i * 256, 256), 256)
        value = mm(u_ref[...], full[i])
        gate = jax.nn.sigmoid(mm(u_ref[...], full[i + ny]))
        gated = (value * gate).astype(BF).astype(F32)
        gated_ref[:, cols] = jnp.where(mask(ROWS, 256), gated, 0.0)
        grad = eg_ref[:, cols].astype(F32) * gate
        em[i] = grad.astype(BF)
        em[i + ny] = (grad * value * (1.0 - gate)).astype(BF)
        return carry

    lax.fori_loop(0, width // 256, gates, 0)

    def tap_grads(i, carry):
        cols = pl.ds(pl.multiple_of(i * 128, 128), 128)
        c = cot_block(cols)
        gated = gated_ref[:, cols]
        sums_k = []
        for k in range(2 * half + 1):
            shifted = pltpu.roll(c, (k - half) % ROWS, 0) if k != half else c
            sums_k.append(jnp.sum(gated * shifted, axis=0, keepdims=True))
        sums_k.append(jnp.zeros((16 - len(sums_k), 128), F32))
        small[:, cols] = jnp.concatenate(sums_k, axis=0)
        return carry

    lax.fori_loop(0, width // 128, tap_grads, 0)

    def unproject(i, carry):
        cols = pl.multiple_of(i * 256, 256)
        total = mm_nt(em[0], full[0, pl.ds(cols, 256), :])
        for t in range(1, tm_n):
            total = total + mm_nt(em[t], full[t, pl.ds(cols, 256), :])
        du_ref[:, pl.ds(cols, 256)] = total
        return carry

    lax.fori_loop(0, width // 256, unproject, 0)
    sums[...] = jnp.zeros_like(sums)

    def denormalise(i, carry):
        rows = pl.ds(pl.multiple_of(i * STEP, STEP), STEP)
        du = du_ref[rows, :]
        n = n_ref[rows, :]
        sums[0:1, :] += jnp.sum(du * n, axis=0, keepdims=True)
        sums[1:2, :] += jnp.sum(du, axis=0, keepdims=True)
        e = du * gain[...]
        e_mean = jnp.mean(e, axis=-1, keepdims=True)
        en_mean = jnp.mean(e * n, axis=-1, keepdims=True)
        dh_ref[rows, :] = (inv_ref[rows, 0:1] * (e - e_mean - n * en_mean)).astype(BF)
        return carry

    lax.fori_loop(0, ROWS // STEP, denormalise, 0)
    small[2 * half + 1 : 2 * half + 3, :] = sums[0:2, :]

    def lin_grad(i, carry):
        cols = pl.ds(pl.multiple_of(i * 256, 256), 256)
        g_lin[:, cols] = mm_tn(a3[...], dh_ref[:, cols])
        return carry

    lax.fori_loop(0, width // 256, lin_grad, 0)

    def later(v):
        return pltpu.roll(v.astype(F32), ROWS - 1, 0)

    ez3 = through_silu(mm_nt(dh_ref[...], lin[...]), z3[...])
    three[256:, :] = mm_tn(a2[...], ez3)
    three[:256, :] = mm_tn(a2[:, 256:], later(ez3).astype(BF))
    first = through_silu(mm_nt(ez3, w_three[256:512, :]), z2[:, :256])
    over = later(mm_nt(ez3, w_three[:256, :]))
    second = through_silu(mm_nt(ez3, w_three[512:, :]) + over, z2[:, 256:])
    side = mm_tn(a1[:, 256:], second)
    two[:256, :] = mm_tn(a1[:, 768:], later(first).astype(BF)) + side[:256]
    two[256:, :] = mm_tn(a1[:, :512], first) + side[256:]
    da = (
        mm_nt(first, w_two[256:512, :]),
        mm_nt(first, w_two[512:, :]) + mm_nt(second, w_two[:256, :]),
        mm_nt(second, w_two[256:512, :]),
        mm_nt(second, w_two[512:, :]) + later(mm_nt(first, w_two[:256, :])),
    )
    tops = (0, 80, 112, 16)
    total = None
    for j in (1, 2, 3):
        low, high = windows[j]
        ez = through_silu(da[j], z1[:, 256 * j : 256 * j + 256])
        term = mm_tn(xw[:, low:high], ez)[tops[j] : tops[j] + 240]
        total = term if total is None else total + term
    ez = through_silu(da[0], z1[:, :256])
    here = mm_tn(xw[:, :256], ez)[:160]
    gone = mm_tn(xw[:, 640:768], ez)[48:]
    one[...] = total + jnp.concatenate([gone, here], axis=0)
    for copy in started:
        copy.wait_send()


def work(operands, tm_n, half, block_rows, scale):
    proj, lin = operands[3], operands[7]
    width = lin.shape[1]
    vmem = pl.BlockSpec(memory_space=pltpu.VMEM)
    ny = tm_n // CORES
    copies = 2 + 2 * (ny - 1) + 1

    def buf(*shape, dtype=BF):
        return pltpu.VMEM(shape, dtype)

    return pl.pallas_call(
        functools.partial(work_kernel, tm_n, half, block_rows, scale),
        out_shape=[
            jax.ShapeDtypeStruct(shape, F32)
            for shape in ((240, 256), (768, 256), (768, 256), (256, width), (16, width))
        ],
        in_specs=[pl.BlockSpec(memory_space=pltpu.SMEM)] + [vmem] * 10,
        out_specs=[vmem] * 5,
        scratch_shapes=[
            buf(tm_n, *proj.shape),
            buf(768, 1024),
            buf(ROWS, 768),
            buf(RIM, 640),
            buf(RIM, 640),
            buf(RIM, 640),
            buf(ROWS, 1024, dtype=F32),
            buf(ROWS, 512, dtype=F32),
            buf(ROWS, 256, dtype=F32),
            buf(ROWS, 1024),
            buf(ROWS, 512),
            buf(ROWS, 256),
            buf(ROWS, width, dtype=F32),
            buf(ROWS, 128, dtype=F32),
            buf(ROWS, width),
            buf(ROWS, width, dtype=F32),
            buf(ROWS, width),
            buf(ROWS, width, dtype=F32),
            buf(tm_n, ROWS, 256),
            buf(ROWS, width),
            buf(8, width, dtype=F32),
            pltpu.SemaphoreType.DMA,
            pltpu.SemaphoreType.DMA((copies,)),
            pltpu.SemaphoreType.DMA((copies,)),
        ],
        compiler_params=pltpu.CompilerParams(
            collective_id=1, has_side_effects=True, vmem_limit_bytes=56 * 1024 * 1024
        ),
    )(*operands)


def per_device(
    mel,
    cotangent,
    conv_one,
    conv_two,
    conv_three,
    linear_weight,
    ln_gain,
    ln_bias,
    proj,
    dw_kernel,
    blocks,
):
    tm_count = lax.axis_size("tm")
    dp_count = lax.axis_size("dp")
    block_rows = mel.shape[1] // dp_count
    taps = dw_kernel.shape[0]
    total_rows = (dp_count * dp_count + 2) // 3 * block_rows * tm_count
    results = work(
        (
            blocks,
            mel,
            cotangent,
            proj,
            conv_one,
            conv_two,
            conv_three,
            linear_weight,
            ln_gain[None],
            ln_bias[None],
            dw_kernel,
        ),
        tm_count,
        taps // 2,
        block_rows,
        total_rows**-0.5,
    )
    one, two, three, lin, small = sum_everywhere(results, dp_count // NX, tm_count // CORES)
    return (one, two, three, lin, small[taps], small[taps + 1], small[:taps])


def solution(mesh):
    return jax.shard_map(
        per_device,
        mesh=mesh,
        in_specs=(
            P("dp", "tm", None),
            P("dp", "tm", None),
            P(),
            P(),
            P(),
            P(),
            P(),
            P(),
            P(None, "tm"),
            P(),
            P(),
        ),
        out_specs=(P(), P(), P(), P(), P(), P(), P()),
        check_vma=False,
    )
```

```python
import functools

import jax
import jax.numpy as jnp
from jax import lax
from jax.experimental import pallas as pl
from jax.experimental.pallas import tpu as pltpu
from jax.sharding import PartitionSpec as P

EPSILON = 1e-05
BF = jnp.bfloat16
F32 = jnp.float32


def mm(lhs, rhs):
    return jnp.dot(lhs, rhs, preferred_element_type=F32)


def mm_tn(lhs, rhs):
    return lax.dot_general(lhs, rhs, (((0,), (0,)), ((), ())), preferred_element_type=F32)


def mm_nt(lhs, rhs):
    return lax.dot_general(lhs, rhs, (((1,), (1,)), ((), ())), preferred_element_type=F32)


def silu(z):
    return (z * jax.nn.sigmoid(z)).astype(BF)


def through_silu(grad, z):
    s = jax.nn.sigmoid(z)
    return (grad * (s * (1.0 + z * (1.0 - s)))).astype(BF)


NX = 4
CORES = 2
PIECE = 48
LANES = 256
SUB = 8


def row_loop(count, step, body):
    lax.fori_loop(0, count // step, lambda i, carry: (body(pl.multiple_of(i * step, step)), carry)[1], 0)


def sum_kernel(
    nz, ny, one, two, three, lin, small, result,
    acc, out, snd, from_core, from_first, from_second, z_acc, z_snd, from_z, z_out,
    send_sem, recv_sem,
):
    dp, tm = lax.axis_index("dp"), lax.axis_index("tm")
    z, x = dp // NX, dp % NX
    y, core = tm // CORES, tm % CORES
    fan = NX
    chunk = fan * PIECE
    half = fan * chunk

    def at_y(d):
        return (dp, ((y + d) % ny) * CORES + core)

    def at_x(d):
        return (z * NX + (x + d) % NX, tm)

    def at_z(d):
        return (((z + d) % nz) * NX + x, tm)

    at_core = (dp, y * CORES + (1 - core))
    colours = ((0, y, at_y, x, at_x), (1, x, at_x, y, at_y))

    barrier = pltpu.get_barrier_semaphore()
    peers = [at_z(d) for d in range(1, nz)] + [at_x(d) for d in range(1, NX)]
    peers = peers + [at_y(d) for d in range(1, ny)] + [at_core]
    for peer in peers:
        pl.semaphore_signal(barrier, inc=1, device_id=peer, device_id_type=pl.DeviceIdType.MESH)

    top = 0
    for src in (one, two, three, lin, small):
        for lane in range(0, src.shape[1], LANES):
            step = 16 if src.shape[0] % 48 else 48

            def fill(i, src=src, lane=lane, top=top, step=step):
                acc[pl.ds(top + i, step), :] = src[pl.ds(i, step), pl.ds(lane, LANES)]

            row_loop(src.shape[0], step, fill)
            top += src.shape[0]
    rest = acc.shape[0] - top
    acc[pl.ds(top, rest), :] = jnp.zeros((rest, LANES), F32)

    started = []

    def send(src, dst, peer):
        k = len(started)
        copy = pltpu.make_async_remote_copy(
            src_ref=src,
            dst_ref=dst,
            send_sem=send_sem.at[k],
            recv_sem=recv_sem.at[k],
            device_id=peer,
            device_id_type=pl.DeviceIdType.MESH,
        )
        copy.start()
        started.append(copy)
        return copy

    def mine(colour):
        return (colour * CORES + core) * half

    def theirs(colour):
        return (colour * CORES + 1 - core) * half

    order = list(range(1, fan)) + [0]
    pl.semaphore_wait(barrier, len(peers))
    core_copies = []
    for d in order:
        for colour, first, _, _, _ in colours:
            place = ((first + d) % fan) * chunk

            def narrow(i, place=place, colour=colour):
                at = pl.multiple_of(theirs(colour) + place + i, PIECE)
                snd[pl.ds(at, PIECE), :] = acc[pl.ds(at, PIECE), :].astype(BF)

            row_loop(chunk, PIECE, narrow)
            core_copies.append(
                send(
                    snd.at[pl.ds(pl.multiple_of(theirs(colour) + place, PIECE), chunk)],
                    from_core.at[pl.ds(pl.multiple_of(colour * half + place, PIECE), chunk)],
                    at_core,
                )
            )
    first_copies = []
    for d in order:
        for colour, first, at_first, _, _ in colours:
            core_copies.pop(0).wait_recv()
            place = ((first + d) % fan) * chunk

            def add_core(i, place=place, d=d, colour=colour):
                at = pl.multiple_of(mine(colour) + place + i, PIECE)
                came = from_core[pl.ds(pl.multiple_of(colour * half + place + i, PIECE), PIECE), :]
                total = acc[pl.ds(at, PIECE), :] + came.astype(F32)
                if d == 0:
                    acc[pl.ds(at, PIECE), :] = total
                else:
                    snd[pl.ds(at, PIECE), :] = total.astype(BF)

            row_loop(chunk, PIECE, add_core)
            if d:
                at = pl.multiple_of(mine(colour) + place, PIECE)
                first_copies.append(
                    send(snd.at[pl.ds(at, chunk)], from_first.at[colour, d - 1], at_first(d))
                )
    for copy in first_copies:
        copy.wait_recv()
    second_copies = []
    for colour, first, _, second, at_second in colours:
        own = mine(colour) + first * chunk

        def add_first(i, own=own, colour=colour):
            at = pl.multiple_of(own + i, PIECE)
            total = acc[pl.ds(at, PIECE), :]
            for d in range(1, fan):
                total = total + from_first[colour, d - 1, pl.ds(i, PIECE), :].astype(F32)
            acc[pl.ds(at, PIECE), :] = total
            snd[pl.ds(at, PIECE), :] = total.astype(BF)

        row_loop(chunk, PIECE, add_first)
        for d in range(1, fan):
            at = pl.multiple_of(own + ((second + d) % fan) * PIECE, PIECE)
            second_copies.append(
                send(snd.at[pl.ds(at, PIECE)], from_second.at[colour, d - 1], at_second(d))
            )
    parts = PIECE // SUB
    for colour, first, _, second, _ in colours:
        for _ in range(1, fan):
            second_copies.pop(0).wait_recv()
        piece = pl.multiple_of(mine(colour) + first * chunk + second * PIECE, PIECE)
        total = acc[pl.ds(piece, PIECE), :]
        for d in range(1, fan):
            total = total + from_second[colour, d - 1].astype(F32)
        total = total.reshape(parts, SUB, LANES)
        z_acc[pl.ds(colour * parts, parts)] = total
        z_snd[pl.ds(colour * parts, parts)] = total.astype(BF)
    used = 2 * parts
    z_acc[pl.ds(used, nz - used)] = jnp.zeros((nz - used, SUB, LANES), F32)
    z_snd[pl.ds(used, nz - used)] = jnp.zeros((nz - used, SUB, LANES), BF)
    far = sorted(range(1, nz), key=lambda d: -min(d, nz - d))
    z_copies = [send(z_snd.at[(z + d) % nz], from_z.at[d - 1], at_z(d)) for d in far]
    for copy in z_copies:
        copy.wait_recv()
    total = z_acc[z]
    for d in range(1, nz):
        total = total + from_z[d - 1].astype(F32)
    z_out[z] = total.astype(BF)
    z_copies = [send(z_out.at[z], z_out.at[z], at_z(d)) for d in far]
    for copy in z_copies:
        copy.wait_recv()
    for colour, first, _, second, at_second in colours:
        done = z_out[pl.ds(colour * parts, parts)].astype(F32).reshape(PIECE, LANES)
        piece = pl.multiple_of(mine(colour) + first * chunk + second * PIECE, PIECE)
        out[pl.ds(piece, PIECE), :] = done.astype(BF)
        whole = out.at[pl.ds(piece, PIECE)]
        second_copies.extend([send(whole, whole, at_second(d)) for d in range(1, fan)])
    for copy in second_copies:
        copy.wait_recv()
    first_copies = []
    for colour, first, at_first, _, _ in colours:
        whole = out.at[pl.ds(pl.multiple_of(mine(colour) + first * chunk, PIECE), chunk)]
        first_copies.append([send(whole, whole, at_first(d)) for d in range(1, fan)])
        core_copies.append(send(whole, whole, at_core))
    for d in range(1, fan):
        for colour, first, _, _, _ in colours:
            first_copies[colour][d - 1].wait_recv()
            place = pl.multiple_of(mine(colour) + ((first - d + fan) % fan) * chunk, PIECE)
            whole = out.at[pl.ds(place, chunk)]
            core_copies.append(send(whole, whole, at_core))
    for copy in core_copies:
        copy.wait_recv()

    def drain(i):
        result[pl.ds(i, PIECE), :] = out[pl.ds(i, PIECE), :]

    row_loop(out.shape[0], PIECE, drain)
    for copy in started:
        copy.wait_send()


def unpack_kernel(packed, one, two, three, lin, small):
    top = 0
    for dst in (one, two, three, lin, small):
        for lane in range(0, dst.shape[1], LANES):
            step = 16 if dst.shape[0] % 48 else 48

            def drain(i, dst=dst, lane=lane, top=top, step=step):
                dst[pl.ds(i, step), pl.ds(lane, LANES)] = packed[pl.ds(top + i, step), :]

            row_loop(dst.shape[0], step, drain)
            top += dst.shape[0]


def sum_everywhere(pieces, nz, ny):
    total = 2 * CORES * NX * NX * PIECE
    copies = 2 * (2 * (NX + 2 * (NX - 1)) + nz - 1)
    vmem = pl.BlockSpec(memory_space=pltpu.VMEM)
    packed = pl.pallas_call(
        functools.partial(sum_kernel, nz, ny),
        out_shape=jax.ShapeDtypeStruct((total, LANES), BF),
        in_specs=[vmem] * len(pieces),
        out_specs=vmem,
        scratch_shapes=[
            pltpu.VMEM((total, LANES), F32),
            pltpu.VMEM((total, LANES), BF),
            pltpu.VMEM((total, LANES), BF),
            pltpu.VMEM((total // CORES, LANES), BF),
            pltpu.VMEM((2, NX - 1, NX * PIECE, LANES), BF),
            pltpu.VMEM((2, NX - 1, PIECE, LANES), BF),
            pltpu.VMEM((nz, SUB, LANES), F32),
            pltpu.VMEM((nz, SUB, LANES), BF),
            pltpu.VMEM((nz - 1, SUB, LANES), BF),
            pltpu.VMEM((nz, SUB, LANES), BF),
            pltpu.SemaphoreType.DMA((copies,)),
            pltpu.SemaphoreType.DMA((copies,)),
        ],
        compiler_params=pltpu.CompilerParams(collective_id=0, has_side_effects=True),
    )(*pieces)
    return pl.pallas_call(
        unpack_kernel,
        out_shape=[jax.ShapeDtypeStruct(p.shape, BF) for p in pieces],
        in_specs=[vmem],
        out_specs=[vmem] * len(pieces),
    )(packed)


ROWS = 336
STEP = 48
RIM = 16
DIRECT = 256
X_PART = 96
Z_PART = 192


def work_kernel(
    tm_n, half, block_rows, scale, blocks, mel_ref, cot_ref, proj, conv_one, w_two, w_three, lin, gain, bias, taps,
    one, two, three, g_lin, small,
    full, w_one, xw, up_snd, up_rcv, down_rcv, z1, z2, z3, a1, a2, a3, n_ref, inv_ref, u_ref, du_ref,
    eg_ref, gated_ref, em, dh_ref, sums, own_sem, send_sem, recv_sem,
):
    dp, tm = lax.axis_index("dp"), lax.axis_index("tm")
    ny = tm_n // CORES
    y, core = tm // CORES, tm % CORES
    depth, x = dp // NX, dp % NX
    mel, cot = mel_ref.at[0], cot_ref.at[0]
    own_rows = mel.shape[0]
    width = lin.shape[1]
    live = blocks[dp] * block_rows

    def at(d):
        return (dp, (tm + d) % tm_n)

    def at_x(d):
        return (depth * NX + (x + d) % NX, tm)

    at_z = ((depth + 1 - 2 * (depth % 2)) * NX + x, tm)
    barrier = pltpu.get_barrier_semaphore()
    peers = [at(d) for d in range(1, tm_n)] + [at_x(d) for d in range(1, NX)] + [at_z]
    for peer in peers:
        pl.semaphore_signal(barrier, inc=1, device_id=peer, device_id_type=pl.DeviceIdType.MESH)

    first_row = lax.broadcasted_iota(jnp.int32, (RIM, own_rows), 0)
    column = lax.broadcasted_iota(jnp.int32, (RIM, own_rows), 1)
    pick = (column - live == first_row - RIM) & (first_row >= RIM - half - 1)
    up_snd[...] = mm(pick.astype(F32).astype(BF), mel[...]).astype(BF)
    bins = conv_one.shape[0] // 3

    def clear(i):
        w_one[pl.ds(i, 48), :] = jnp.zeros((48, 1024), BF)

    row_loop(768, 48, clear)
    w_one[: 2 * bins, :256] = conv_one[bins:, :]
    w_one[768 - bins :, :256] = conv_one[:bins, :]
    for j in range(1, 4):
        above = (2 * j - 1) * bins
        w_one[above : above + 3 * bins, 256 * j : 256 * j + 256] = conv_one[...]
    pl.semaphore_wait(barrier, len(peers))

    started = []

    def send(src, dst, peer):
        k = len(started)
        copy = pltpu.make_async_remote_copy(
            src_ref=src,
            dst_ref=dst,
            send_sem=send_sem.at[k],
            recv_sem=recv_sem.at[k],
            device_id=peer,
            device_id_type=pl.DeviceIdType.MESH,
        )
        copy.start()
        started.append(copy)
        return copy

    partner = (dp, y * CORES + (1 - core))
    up = send(up_snd, up_rcv, at(1))
    down = send(mel.at[pl.ds(0, RIM)], down_rcv, at(tm_n - 1))
    direct = pl.ds(0, DIRECT)

    def x_part(q):
        return pl.ds(pl.multiple_of(DIRECT + q * X_PART, 16), X_PART)

    def z_part(q):
        return pl.ds(pl.multiple_of(DIRECT + NX * X_PART + q * Z_PART, 16), Z_PART)

    def pass_on(came, part, peer):
        return send(full.at[came, part], full.at[came, part], peer)

    near = (1, 3, 2)
    y_copies = {}
    for name, part in (("x", x_part(x)), ("z", z_part(depth % 2)), ("direct", direct)):
        for d in near:
            peer = (dp, ((y + d) % ny) * CORES + core)
            y_copies[name, d] = send(proj.at[part], full.at[tm, part], peer)
    core_copies = [send(proj, full.at[tm], partner)]
    came = {d: ((y - d + ny) % ny) * CORES + core for d in near}
    x_copies = {}
    z_copies = {}
    keep = pltpu.make_async_copy(proj, full.at[tm], own_sem)
    keep.start()

    def mask(count, lanes):
        ids = lax.broadcasted_iota(jnp.int32, (count, lanes), 0)
        right = (ids < live + half) & (tm < tm_n - 1)
        left = (ids >= ROWS - half) & (tm > 0)
        return (ids < live) | right | left

    def cot_block(cols):
        c = cot[:, cols].astype(F32) * scale
        ids = lax.broadcasted_iota(jnp.int32, c.shape, 0)
        c = jnp.where(ids < live, c, 0.0)
        return jnp.concatenate([c, jnp.zeros((ROWS - own_rows, c.shape[1]), F32)], axis=0)

    def back_taps(i, carry):
        cols = pl.ds(pl.multiple_of(i * 128, 128), 128)
        c = cot_block(cols)
        total = jnp.zeros_like(c)
        weights = taps[:, cols].astype(F32)
        for k in range(2 * half + 1):
            shifted = pltpu.roll(c, (k - half) % ROWS, 0) if k != half else c
            total = total + shifted * weights[k : k + 1]
        eg_ref[:, cols] = jnp.where(mask(ROWS, 128), total, 0.0).astype(BF)
        return carry

    lax.fori_loop(0, width // 128, back_taps, 0)

    up.wait_recv()
    down.wait_recv()

    def place(i, carry):
        at_row = pl.multiple_of(i * 64, 64)
        rows = lax.broadcasted_iota(jnp.int32, (64, RIM), 0) + at_row
        slot = lax.broadcasted_iota(jnp.int32, (64, RIM), 1)
        pick = (rows - live == slot) & (slot < half) & (tm < tm_n - 1)
        ids = lax.broadcasted_iota(jnp.int32, (64, mel.shape[1]), 0) + at_row
        value = jnp.where(ids < live, mel[pl.ds(at_row, 64), :].astype(F32), 0.0)
        value = value + mm(pick.astype(F32).astype(BF), down_rcv[...])
        xw[pl.ds(at_row, 64), 0:640] = value.astype(BF)
        return carry

    lax.fori_loop(0, own_rows // 64, place, 0)
    rows = lax.broadcasted_iota(jnp.int32, (RIM, RIM), 0) + own_rows
    slot = lax.broadcasted_iota(jnp.int32, (RIM, RIM), 1)
    pick = (rows - live == slot) & (slot < half) & (tm < tm_n - 1)
    value = mm(pick.astype(F32).astype(BF), down_rcv[...])
    value = value + jnp.where(tm > 0, 1.0, 0.0) * up_rcv[...].astype(F32)
    xw[own_rows:ROWS, 0:640] = value.astype(BF)
    xw[:, 640:768] = pltpu.roll(xw[:, 512:640].astype(F32), 1, 0).astype(BF)

    windows = ((0, 256), (0, 384), (128, 512), (384, 640))
    for j, (low, high) in enumerate(windows):
        cols = slice(256 * j, 256 * j + 256)
        z = mm(xw[:, low:high], w_one[low:high, cols])
        if j == 0:
            z = z + mm(xw[:, 640:768], w_one[640:768, cols])
        z1[:, cols] = z
        a1[:, cols] = silu(z)
    z = mm(a1[:, :512], w_two[256:, :]) + pltpu.roll(mm(a1[:, 768:], w_two[:256, :]), 1, 0)
    z2[:, :256] = z
    a2[:, :256] = silu(z)
    z = mm(a1[:, 256:], w_two[...])
    z2[:, 256:] = z
    a2[:, 256:] = silu(z)
    z = mm(a2[...], w_three[256:, :]) + pltpu.roll(mm(a2[:, 256:], w_three[:256, :]), 1, 0)
    z3[...] = z
    a3[...] = silu(z)

    for d in near:
        y_copies["x", d].wait_recv()
        for far in range(1, NX):
            x_copies[d, far] = pass_on(came[d], x_part(x), at_x(far))
    for d in near:
        core_copies.append(pass_on(came[d], x_part(x), partner))

    def project(i, carry):
        cols = pl.ds(pl.multiple_of(i * 256, 256), 256)
        n_ref[:, cols] = mm(a3[...], lin[:, cols]).astype(BF).astype(F32)
        return carry

    lax.fori_loop(0, width // 256, project, 0)

    def normalise(i, carry):
        rows = pl.ds(pl.multiple_of(i * STEP, STEP), STEP)
        h = n_ref[rows, :]
        h = h - jnp.mean(h, axis=-1, keepdims=True)
        inverse = lax.rsqrt(jnp.mean(h * h, axis=-1, keepdims=True) + EPSILON)
        n = h * inverse
        n_ref[rows, :] = n
        inv_ref[rows, :] = jnp.broadcast_to(inverse, (STEP, 128))
        u_ref[rows, :] = (n * gain[...] + bias[...]).astype(BF)
        return carry

    lax.fori_loop(0, ROWS // STEP, normalise, 0)

    for d in near:
        y_copies["z", d].wait_recv()
        z_copies[d] = pass_on(came[d], z_part(depth % 2), at_z)
        core_copies.append(pass_on(came[d], z_part(depth % 2), partner))
    for d in near:
        y_copies["direct", d].wait_recv()
        core_copies.append(pass_on(came[d], direct, partner))
    for d in near:
        for far in range(1, NX):
            x_copies[d, far].wait_recv()
            core_copies.append(pass_on(came[d], x_part((x - far + NX) % NX), partner))
    for d in near:
        z_copies[d].wait_recv()
        core_copies.append(pass_on(came[d], z_part(1 - depth % 2), partner))
    keep.wait()
    for copy in core_copies:
        copy.wait_recv()

    def gates(i, carry):
        cols = pl.ds(pl.multiple_of(i * 256, 256), 256)
        value = mm(u_ref[...], full[i])
        gate = jax.nn.sigmoid(mm(u_ref[...], full[i + ny]))
        gated = (value * gate).astype(BF).astype(F32)
        gated_ref[:, cols] = jnp.where(mask(ROWS, 256), gated, 0.0)
        grad = eg_ref[:, cols].astype(F32) * gate
        em[i] = grad.astype(BF)
        em[i + ny] = (grad * value * (1.0 - gate)).astype(BF)
        return carry

    lax.fori_loop(0, width // 256, gates, 0)

    def tap_grads(i, carry):
        cols = pl.ds(pl.multiple_of(i * 128, 128), 128)
        c = cot_block(cols)
        gated = gated_ref[:, cols]
        sums_k = []
        for k in range(2 * half + 1):
            shifted = pltpu.roll(c, (k - half) % ROWS, 0) if k != half else c
            sums_k.append(jnp.sum(gated * shifted, axis=0, keepdims=True))
        sums_k.append(jnp.zeros((16 - len(sums_k), 128), F32))
        small[:, cols] = jnp.concatenate(sums_k, axis=0)
        return carry

    lax.fori_loop(0, width // 128, tap_grads, 0)

    def unproject(i, carry):
        cols = pl.multiple_of(i * 256, 256)
        total = mm_nt(em[0], full[0, pl.ds(cols, 256), :])
        for t in range(1, tm_n):
            total = total + mm_nt(em[t], full[t, pl.ds(cols, 256), :])
        du_ref[:, pl.ds(cols, 256)] = total
        return carry

    lax.fori_loop(0, width // 256, unproject, 0)
    sums[...] = jnp.zeros_like(sums)

    def denormalise(i, carry):
        rows = pl.ds(pl.multiple_of(i * STEP, STEP), STEP)
        du = du_ref[rows, :]
        n = n_ref[rows, :]
        sums[0:1, :] += jnp.sum(du * n, axis=0, keepdims=True)
        sums[1:2, :] += jnp.sum(du, axis=0, keepdims=True)
        e = du * gain[...]
        e_mean = jnp.mean(e, axis=-1, keepdims=True)
        en_mean = jnp.mean(e * n, axis=-1, keepdims=True)
        dh_ref[rows, :] = (inv_ref[rows, 0:1] * (e - e_mean - n * en_mean)).astype(BF)
        return carry

    lax.fori_loop(0, ROWS // STEP, denormalise, 0)
    small[2 * half + 1 : 2 * half + 3, :] = sums[0:2, :]

    def lin_grad(i, carry):
        cols = pl.ds(pl.multiple_of(i * 256, 256), 256)
        g_lin[:, cols] = mm_tn(a3[...], dh_ref[:, cols])
        return carry

    lax.fori_loop(0, width // 256, lin_grad, 0)

    def later(v):
        return pltpu.roll(v.astype(F32), ROWS - 1, 0)

    ez3 = through_silu(mm_nt(dh_ref[...], lin[...]), z3[...])
    three[256:, :] = mm_tn(a2[...], ez3)
    three[:256, :] = mm_tn(a2[:, 256:], later(ez3).astype(BF))
    first = through_silu(mm_nt(ez3, w_three[256:512, :]), z2[:, :256])
    over = later(mm_nt(ez3, w_three[:256, :]))
    second = through_silu(mm_nt(ez3, w_three[512:, :]) + over, z2[:, 256:])
    side = mm_tn(a1[:, 256:], second)
    two[:256, :] = mm_tn(a1[:, 768:], later(first).astype(BF)) + side[:256]
    two[256:, :] = mm_tn(a1[:, :512], first) + side[256:]
    da = (
        mm_nt(first, w_two[256:512, :]),
        mm_nt(first, w_two[512:, :]) + mm_nt(second, w_two[:256, :]),
        mm_nt(second, w_two[256:512, :]),
        mm_nt(second, w_two[512:, :]) + later(mm_nt(first, w_two[:256, :])),
    )
    tops = (0, 80, 112, 16)
    total = None
    for j in (1, 2, 3):
        low, high = windows[j]
        ez = through_silu(da[j], z1[:, 256 * j : 256 * j + 256])
        term = mm_tn(xw[:, low:high], ez)[tops[j] : tops[j] + 240]
        total = term if total is None else total + term
    ez = through_silu(da[0], z1[:, :256])
    here = mm_tn(xw[:, :256], ez)[:160]
    gone = mm_tn(xw[:, 640:768], ez)[48:]
    one[...] = total + jnp.concatenate([gone, here], axis=0)
    for copy in started:
        copy.wait_send()


def work(operands, tm_n, half, block_rows, scale):
    proj, lin = operands[3], operands[7]
    width = lin.shape[1]
    vmem = pl.BlockSpec(memory_space=pltpu.VMEM)
    ny = tm_n // CORES
    copies = 3 + (ny - 1) * (3 + (NX - 1) + 1 + 3 + (NX - 1) + 1)

    def buf(*shape, dtype=BF):
        return pltpu.VMEM(shape, dtype)

    return pl.pallas_call(
        functools.partial(work_kernel, tm_n, half, block_rows, scale),
        out_shape=[
            jax.ShapeDtypeStruct(shape, F32)
            for shape in ((240, 256), (768, 256), (768, 256), (256, width), (16, width))
        ],
        in_specs=[pl.BlockSpec(memory_space=pltpu.SMEM)] + [vmem] * 10,
        out_specs=[vmem] * 5,
        scratch_shapes=[
            buf(tm_n, *proj.shape),
            buf(768, 1024),
            buf(ROWS, 768),
            buf(RIM, 640),
            buf(RIM, 640),
            buf(RIM, 640),
            buf(ROWS, 1024, dtype=F32),
            buf(ROWS, 512, dtype=F32),
            buf(ROWS, 256, dtype=F32),
            buf(ROWS, 1024),
            buf(ROWS, 512),
            buf(ROWS, 256),
            buf(ROWS, width, dtype=F32),
            buf(ROWS, 128, dtype=F32),
            buf(ROWS, width),
            buf(ROWS, width, dtype=F32),
            buf(ROWS, width),
            buf(ROWS, width, dtype=F32),
            buf(tm_n, ROWS, 256),
            buf(ROWS, width),
            buf(8, width, dtype=F32),
            pltpu.SemaphoreType.DMA,
            pltpu.SemaphoreType.DMA((copies,)),
            pltpu.SemaphoreType.DMA((copies,)),
        ],
        compiler_params=pltpu.CompilerParams(
            collective_id=1, has_side_effects=True, vmem_limit_bytes=56 * 1024 * 1024
        ),
    )(*operands)


def per_device(
    mel,
    cotangent,
    conv_one,
    conv_two,
    conv_three,
    linear_weight,
    ln_gain,
    ln_bias,
    proj,
    dw_kernel,
    blocks,
):
    tm_count = lax.axis_size("tm")
    dp_count = lax.axis_size("dp")
    block_rows = mel.shape[1] // dp_count
    taps = dw_kernel.shape[0]
    total_rows = (dp_count * dp_count + 2) // 3 * block_rows * tm_count
    results = work(
        (
            blocks,
            mel,
            cotangent,
            proj,
            conv_one,
            conv_two,
            conv_three,
            linear_weight,
            ln_gain[None],
            ln_bias[None],
            dw_kernel,
        ),
        tm_count,
        taps // 2,
        block_rows,
        total_rows**-0.5,
    )
    one, two, three, lin, small = sum_everywhere(results, dp_count // NX, tm_count // CORES)
    return (one, two, three, lin, small[taps], small[taps + 1], small[:taps])


def solution(mesh):
    return jax.shard_map(
        per_device,
        mesh=mesh,
        in_specs=(
            P("dp", "tm", None),
            P("dp", "tm", None),
            P(),
            P(),
            P(),
            P(),
            P(),
            P(),
            P(None, "tm"),
            P(),
            P(),
        ),
        out_specs=(P(), P(), P(), P(), P(), P(), P()),
        check_vma=False,
    )
```

```python
import functools

import jax
import jax.numpy as jnp
from jax import lax
from jax.experimental import pallas as pl
from jax.experimental.pallas import tpu as pltpu
from jax.sharding import PartitionSpec as P

EPSILON = 1e-05
BF = jnp.bfloat16
F32 = jnp.float32


def mm(lhs, rhs):
    return jnp.dot(lhs, rhs, preferred_element_type=F32)


def mm_tn(lhs, rhs):
    return lax.dot_general(lhs, rhs, (((0,), (0,)), ((), ())), preferred_element_type=F32)


def mm_nt(lhs, rhs):
    return lax.dot_general(lhs, rhs, (((1,), (1,)), ((), ())), preferred_element_type=F32)


def silu(z):
    return (z * jax.nn.sigmoid(z)).astype(BF)


def through_silu(grad, z):
    s = jax.nn.sigmoid(z)
    return (grad * (s * (1.0 + z * (1.0 - s)))).astype(BF)


NX = 4
CORES = 2
PIECE = 48
LANES = 256
SUB = 8


def row_loop(count, step, body):
    lax.fori_loop(0, count // step, lambda i, carry: (body(pl.multiple_of(i * step, step)), carry)[1], 0)


def sum_kernel(
    nz, ny, one, two, three, lin, small, result,
    acc, out, snd, from_core, from_first, from_second, z_acc, z_snd, from_z, z_out,
    send_sem, recv_sem,
):
    dp, tm = lax.axis_index("dp"), lax.axis_index("tm")
    z, x = dp // NX, dp % NX
    y, core = tm // CORES, tm % CORES
    fan = NX
    chunk = fan * PIECE
    half = fan * chunk

    def at_y(d):
        return (dp, ((y + d) % ny) * CORES + core)

    def at_x(d):
        return (z * NX + (x + d) % NX, tm)

    def at_z(d):
        return (((z + d) % nz) * NX + x, tm)

    at_core = (dp, y * CORES + (1 - core))
    colours = ((0, y, at_y, x, at_x), (1, x, at_x, y, at_y))

    top = 0
    for src in (one, two, three, lin, small):
        for lane in range(0, src.shape[1], LANES):
            step = 16 if src.shape[0] % 48 else 48

            def fill(i, src=src, lane=lane, top=top, step=step):
                acc[pl.ds(top + i, step), :] = src[pl.ds(i, step), pl.ds(lane, LANES)]

            row_loop(src.shape[0], step, fill)
            top += src.shape[0]
    rest = acc.shape[0] - top
    acc[pl.ds(top, rest), :] = jnp.zeros((rest, LANES), F32)

    started = []

    def send(src, dst, peer):
        k = len(started)
        copy = pltpu.make_async_remote_copy(
            src_ref=src,
            dst_ref=dst,
            send_sem=send_sem.at[k],
            recv_sem=recv_sem.at[k],
            device_id=peer,
            device_id_type=pl.DeviceIdType.MESH,
        )
        copy.start()
        started.append(copy)
        return copy

    def mine(colour):
        return (colour * CORES + core) * half

    def theirs(colour):
        return (colour * CORES + 1 - core) * half

    order = list(range(1, fan)) + [0]
    core_copies = []
    for d in order:
        for colour, first, _, _, _ in colours:
            place = ((first + d) % fan) * chunk

            def narrow(i, place=place, colour=colour):
                at = pl.multiple_of(theirs(colour) + place + i, PIECE)
                snd[pl.ds(at, PIECE), :] = acc[pl.ds(at, PIECE), :].astype(BF)

            row_loop(chunk, PIECE, narrow)
            core_copies.append(
                send(
                    snd.at[pl.ds(pl.multiple_of(theirs(colour) + place, PIECE), chunk)],
                    from_core.at[pl.ds(pl.multiple_of(colour * half + place, PIECE), chunk)],
                    at_core,
                )
            )
    first_copies = []
    for d in order:
        for colour, first, at_first, _, _ in colours:
            core_copies.pop(0).wait_recv()
            place = ((first + d) % fan) * chunk

            def add_core(i, place=place, d=d, colour=colour):
                at = pl.multiple_of(mine(colour) + place + i, PIECE)
                came = from_core[pl.ds(pl.multiple_of(colour * half + place + i, PIECE), PIECE), :]
                total = acc[pl.ds(at, PIECE), :] + came.astype(F32)
                if d == 0:
                    acc[pl.ds(at, PIECE), :] = total
                else:
                    snd[pl.ds(at, PIECE), :] = total.astype(BF)

            row_loop(chunk, PIECE, add_core)
            if d:
                at = pl.multiple_of(mine(colour) + place, PIECE)
                first_copies.append(
                    send(snd.at[pl.ds(at, chunk)], from_first.at[colour, d - 1], at_first(d))
                )
    for copy in first_copies:
        copy.wait_recv()
    second_copies = []
    for colour, first, _, second, at_second in colours:
        own = mine(colour) + first * chunk

        def add_first(i, own=own, colour=colour):
            at = pl.multiple_of(own + i, PIECE)
            total = acc[pl.ds(at, PIECE), :]
            for d in range(1, fan):
                total = total + from_first[colour, d - 1, pl.ds(i, PIECE), :].astype(F32)
            acc[pl.ds(at, PIECE), :] = total
            snd[pl.ds(at, PIECE), :] = total.astype(BF)

        row_loop(chunk, PIECE, add_first)
        for d in range(1, fan):
            at = pl.multiple_of(own + ((second + d) % fan) * PIECE, PIECE)
            second_copies.append(
                send(snd.at[pl.ds(at, PIECE)], from_second.at[colour, d - 1], at_second(d))
            )
    parts = PIECE // SUB
    for colour, first, _, second, _ in colours:
        for _ in range(1, fan):
            second_copies.pop(0).wait_recv()
        piece = pl.multiple_of(mine(colour) + first * chunk + second * PIECE, PIECE)
        total = acc[pl.ds(piece, PIECE), :]
        for d in range(1, fan):
            total = total + from_second[colour, d - 1].astype(F32)
        total = total.reshape(parts, SUB, LANES)
        z_acc[pl.ds(colour * parts, parts)] = total
        z_snd[pl.ds(colour * parts, parts)] = total.astype(BF)
    used = 2 * parts
    z_acc[pl.ds(used, nz - used)] = jnp.zeros((nz - used, SUB, LANES), F32)
    z_snd[pl.ds(used, nz - used)] = jnp.zeros((nz - used, SUB, LANES), BF)
    far = sorted(range(1, nz), key=lambda d: -min(d, nz - d))
    z_copies = [send(z_snd.at[(z + d) % nz], from_z.at[d - 1], at_z(d)) for d in far]
    for copy in z_copies:
        copy.wait_recv()
    total = z_acc[z]
    for d in range(1, nz):
        total = total + from_z[d - 1].astype(F32)
    z_out[z] = total.astype(BF)
    z_copies = [send(z_out.at[z], z_out.at[z], at_z(d)) for d in far]
    for copy in z_copies:
        copy.wait_recv()
    for colour, first, _, second, at_second in colours:
        done = z_out[pl.ds(colour * parts, parts)].astype(F32).reshape(PIECE, LANES)
        piece = pl.multiple_of(mine(colour) + first * chunk + second * PIECE, PIECE)
        out[pl.ds(piece, PIECE), :] = done.astype(BF)
        whole = out.at[pl.ds(piece, PIECE)]
        second_copies.extend([send(whole, whole, at_second(d)) for d in range(1, fan)])
    for copy in second_copies:
        copy.wait_recv()
    first_copies = []
    for colour, first, at_first, _, _ in colours:
        whole = out.at[pl.ds(pl.multiple_of(mine(colour) + first * chunk, PIECE), chunk)]
        first_copies.append([send(whole, whole, at_first(d)) for d in range(1, fan)])
        core_copies.append(send(whole, whole, at_core))
    for d in range(1, fan):
        for colour, first, _, _, _ in colours:
            first_copies[colour][d - 1].wait_recv()
            place = pl.multiple_of(mine(colour) + ((first - d + fan) % fan) * chunk, PIECE)
            whole = out.at[pl.ds(place, chunk)]
            core_copies.append(send(whole, whole, at_core))
    for copy in core_copies:
        copy.wait_recv()

    def drain(i):
        result[pl.ds(i, PIECE), :] = out[pl.ds(i, PIECE), :]

    row_loop(out.shape[0], PIECE, drain)
    for copy in started:
        copy.wait_send()


def unpack_kernel(packed, one, two, three, lin, small):
    top = 0
    for dst in (one, two, three, lin, small):
        for lane in range(0, dst.shape[1], LANES):
            step = 16 if dst.shape[0] % 48 else 48

            def drain(i, dst=dst, lane=lane, top=top, step=step):
                dst[pl.ds(i, step), pl.ds(lane, LANES)] = packed[pl.ds(top + i, step), :]

            row_loop(dst.shape[0], step, drain)
            top += dst.shape[0]


def sum_scratch(nz):
    total = 2 * CORES * NX * NX * PIECE
    copies = 2 * (2 * (NX + 2 * (NX - 1)) + nz - 1)
    return [
        pltpu.VMEM((total, LANES), F32),
        pltpu.VMEM((total, LANES), BF),
        pltpu.VMEM((total, LANES), BF),
        pltpu.VMEM((total // CORES, LANES), BF),
        pltpu.VMEM((2, NX - 1, NX * PIECE, LANES), BF),
        pltpu.VMEM((2, NX - 1, PIECE, LANES), BF),
        pltpu.VMEM((nz, SUB, LANES), F32),
        pltpu.VMEM((nz, SUB, LANES), BF),
        pltpu.VMEM((nz - 1, SUB, LANES), BF),
        pltpu.VMEM((nz, SUB, LANES), BF),
        pltpu.SemaphoreType.DMA((copies,)),
        pltpu.SemaphoreType.DMA((copies,)),
    ]


ROWS = 336
STEP = 48
RIM = 16
DIRECT = 256
X_PART = 96
Z_PART = 192


def work_kernel(
    tm_n, half, block_rows, scale, nz, blocks, mel_ref, cot_ref, proj, conv_one, w_two, w_three, lin, gain, bias, taps,
    one, two, three, g_lin, small,
    full, w_one, xw, up_snd, up_rcv, down_rcv, z1, z2, z3, a1, a2, a3, n_ref, inv_ref, u_ref, du_ref,
    eg_ref, gated_ref, em, dh_ref, sums, own_sem, send_sem, recv_sem,
):
    dp, tm = lax.axis_index("dp"), lax.axis_index("tm")
    ny = tm_n // CORES
    y, core = tm // CORES, tm % CORES
    depth, x = dp // NX, dp % NX
    mel, cot = mel_ref.at[0], cot_ref.at[0]
    own_rows = mel.shape[0]
    width = lin.shape[1]
    live = blocks[dp] * block_rows

    def at(d):
        return (dp, (tm + d) % tm_n)

    def at_x(d):
        return (depth * NX + (x + d) % NX, tm)

    at_z = ((depth + 1 - 2 * (depth % 2)) * NX + x, tm)
    barrier = pltpu.get_barrier_semaphore()
    peers = [at(d) for d in range(1, tm_n)] + [at_x(d) for d in range(1, NX)]
    peers = peers + [(((depth + d) % nz) * NX + x, tm) for d in range(1, nz)]
    for peer in peers:
        pl.semaphore_signal(barrier, inc=1, device_id=peer, device_id_type=pl.DeviceIdType.MESH)

    first_row = lax.broadcasted_iota(jnp.int32, (RIM, own_rows), 0)
    column = lax.broadcasted_iota(jnp.int32, (RIM, own_rows), 1)
    pick = (column - live == first_row - RIM) & (first_row >= RIM - half - 1)
    up_snd[...] = mm(pick.astype(F32).astype(BF), mel[...]).astype(BF)
    bins = conv_one.shape[0] // 3

    def clear(i):
        w_one[pl.ds(i, 48), :] = jnp.zeros((48, 1024), BF)

    row_loop(768, 48, clear)
    w_one[: 2 * bins, :256] = conv_one[bins:, :]
    w_one[768 - bins :, :256] = conv_one[:bins, :]
    for j in range(1, 4):
        above = (2 * j - 1) * bins
        w_one[above : above + 3 * bins, 256 * j : 256 * j + 256] = conv_one[...]
    pl.semaphore_wait(barrier, len(peers))

    started = []

    def send(src, dst, peer):
        k = len(started)
        copy = pltpu.make_async_remote_copy(
            src_ref=src,
            dst_ref=dst,
            send_sem=send_sem.at[k],
            recv_sem=recv_sem.at[k],
            device_id=peer,
            device_id_type=pl.DeviceIdType.MESH,
        )
        copy.start()
        started.append(copy)
        return copy

    partner = (dp, y * CORES + (1 - core))
    up = send(up_snd, up_rcv, at(1))
    down = send(mel.at[pl.ds(0, RIM)], down_rcv, at(tm_n - 1))
    direct = pl.ds(0, DIRECT)

    def x_part(q):
        return pl.ds(pl.multiple_of(DIRECT + q * X_PART, 16), X_PART)

    def z_part(q):
        return pl.ds(pl.multiple_of(DIRECT + NX * X_PART + q * Z_PART, 16), Z_PART)

    def pass_on(came, part, peer):
        return send(full.at[came, part], full.at[came, part], peer)

    near = (1, 3, 2)
    y_copies = {}
    for name, part in (("x", x_part(x)), ("z", z_part(depth % 2)), ("direct", direct)):
        for d in near:
            peer = (dp, ((y + d) % ny) * CORES + core)
            y_copies[name, d] = send(proj.at[part], full.at[tm, part], peer)
    core_copies = [send(proj, full.at[tm], partner)]
    came = {d: ((y - d + ny) % ny) * CORES + core for d in near}
    x_copies = {}
    z_copies = {}
    keep = pltpu.make_async_copy(proj, full.at[tm], own_sem)
    keep.start()

    def mask(count, lanes):
        ids = lax.broadcasted_iota(jnp.int32, (count, lanes), 0)
        right = (ids < live + half) & (tm < tm_n - 1)
        left = (ids >= ROWS - half) & (tm > 0)
        return (ids < live) | right | left

    def cot_block(cols):
        c = cot[:, cols].astype(F32) * scale
        ids = lax.broadcasted_iota(jnp.int32, c.shape, 0)
        c = jnp.where(ids < live, c, 0.0)
        return jnp.concatenate([c, jnp.zeros((ROWS - own_rows, c.shape[1]), F32)], axis=0)

    def back_taps(i, carry):
        cols = pl.ds(pl.multiple_of(i * 128, 128), 128)
        c = cot_block(cols)
        total = jnp.zeros_like(c)
        weights = taps[:, cols].astype(F32)
        for k in range(2 * half + 1):
            shifted = pltpu.roll(c, (k - half) % ROWS, 0) if k != half else c
            total = total + shifted * weights[k : k + 1]
        eg_ref[:, cols] = jnp.where(mask(ROWS, 128), total, 0.0).astype(BF)
        return carry

    lax.fori_loop(0, width // 128, back_taps, 0)

    up.wait_recv()
    down.wait_recv()

    def place(i, carry):
        at_row = pl.multiple_of(i * 64, 64)
        rows = lax.broadcasted_iota(jnp.int32, (64, RIM), 0) + at_row
        slot = lax.broadcasted_iota(jnp.int32, (64, RIM), 1)
        pick = (rows - live == slot) & (slot < half) & (tm < tm_n - 1)
        ids = lax.broadcasted_iota(jnp.int32, (64, mel.shape[1]), 0) + at_row
        value = jnp.where(ids < live, mel[pl.ds(at_row, 64), :].astype(F32), 0.0)
        value = value + mm(pick.astype(F32).astype(BF), down_rcv[...])
        xw[pl.ds(at_row, 64), 0:640] = value.astype(BF)
        return carry

    lax.fori_loop(0, own_rows // 64, place, 0)
    rows = lax.broadcasted_iota(jnp.int32, (RIM, RIM), 0) + own_rows
    slot = lax.broadcasted_iota(jnp.int32, (RIM, RIM), 1)
    pick = (rows - live == slot) & (slot < half) & (tm < tm_n - 1)
    value = mm(pick.astype(F32).astype(BF), down_rcv[...])
    value = value + jnp.where(tm > 0, 1.0, 0.0) * up_rcv[...].astype(F32)
    xw[own_rows:ROWS, 0:640] = value.astype(BF)
    xw[:, 640:768] = pltpu.roll(xw[:, 512:640].astype(F32), 1, 0).astype(BF)

    windows = ((0, 256), (0, 384), (128, 512), (384, 640))
    for j, (low, high) in enumerate(windows):
        cols = slice(256 * j, 256 * j + 256)
        z = mm(xw[:, low:high], w_one[low:high, cols])
        if j == 0:
            z = z + mm(xw[:, 640:768], w_one[640:768, cols])
        z1[:, cols] = z
        a1[:, cols] = silu(z)
    z = mm(a1[:, :512], w_two[256:, :]) + pltpu.roll(mm(a1[:, 768:], w_two[:256, :]), 1, 0)
    z2[:, :256] = z
    a2[:, :256] = silu(z)
    z = mm(a1[:, 256:], w_two[...])
    z2[:, 256:] = z
    a2[:, 256:] = silu(z)
    z = mm(a2[...], w_three[256:, :]) + pltpu.roll(mm(a2[:, 256:], w_three[:256, :]), 1, 0)
    z3[...] = z
    a3[...] = silu(z)

    for d in near:
        y_copies["x", d].wait_recv()
        for far in range(1, NX):
            x_copies[d, far] = pass_on(came[d], x_part(x), at_x(far))
    for d in near:
        core_copies.append(pass_on(came[d], x_part(x), partner))

    def project(i, carry):
        cols = pl.ds(pl.multiple_of(i * 256, 256), 256)
        n_ref[:, cols] = mm(a3[...], lin[:, cols]).astype(BF).astype(F32)
        return carry

    lax.fori_loop(0, width // 256, project, 0)

    def normalise(i, carry):
        rows = pl.ds(pl.multiple_of(i * STEP, STEP), STEP)
        h = n_ref[rows, :]
        h = h - jnp.mean(h, axis=-1, keepdims=True)
        inverse = lax.rsqrt(jnp.mean(h * h, axis=-1, keepdims=True) + EPSILON)
        n = h * inverse
        n_ref[rows, :] = n
        inv_ref[rows, :] = jnp.broadcast_to(inverse, (STEP, 128))
        u_ref[rows, :] = (n * gain[...] + bias[...]).astype(BF)
        return carry

    lax.fori_loop(0, ROWS // STEP, normalise, 0)

    for d in near:
        y_copies["z", d].wait_recv()
        z_copies[d] = pass_on(came[d], z_part(depth % 2), at_z)
        core_copies.append(pass_on(came[d], z_part(depth % 2), partner))
    for d in near:
        y_copies["direct", d].wait_recv()
        core_copies.append(pass_on(came[d], direct, partner))
    for d in near:
        for far in range(1, NX):
            x_copies[d, far].wait_recv()
            core_copies.append(pass_on(came[d], x_part((x - far + NX) % NX), partner))
    for d in near:
        z_copies[d].wait_recv()
        core_copies.append(pass_on(came[d], z_part(1 - depth % 2), partner))
    keep.wait()
    for copy in core_copies:
        copy.wait_recv()

    def gates(i, carry):
        cols = pl.ds(pl.multiple_of(i * 256, 256), 256)
        value = mm(u_ref[...], full[i])
        gate = jax.nn.sigmoid(mm(u_ref[...], full[i + ny]))
        gated = (value * gate).astype(BF).astype(F32)
        gated_ref[:, cols] = jnp.where(mask(ROWS, 256), gated, 0.0)
        grad = eg_ref[:, cols].astype(F32) * gate
        em[i] = grad.astype(BF)
        em[i + ny] = (grad * value * (1.0 - gate)).astype(BF)
        return carry

    lax.fori_loop(0, width // 256, gates, 0)

    def tap_grads(i, carry):
        cols = pl.ds(pl.multiple_of(i * 128, 128), 128)
        c = cot_block(cols)
        gated = gated_ref[:, cols]
        sums_k = []
        for k in range(2 * half + 1):
            shifted = pltpu.roll(c, (k - half) % ROWS, 0) if k != half else c
            sums_k.append(jnp.sum(gated * shifted, axis=0, keepdims=True))
        sums_k.append(jnp.zeros((16 - len(sums_k), 128), F32))
        small[:, cols] = jnp.concatenate(sums_k, axis=0)
        return carry

    lax.fori_loop(0, width // 128, tap_grads, 0)

    def unproject(i, carry):
        cols = pl.multiple_of(i * 256, 256)
        total = mm_nt(em[0], full[0, pl.ds(cols, 256), :])
        for t in range(1, tm_n):
            total = total + mm_nt(em[t], full[t, pl.ds(cols, 256), :])
        du_ref[:, pl.ds(cols, 256)] = total
        return carry

    lax.fori_loop(0, width // 256, unproject, 0)
    sums[...] = jnp.zeros_like(sums)

    def denormalise(i, carry):
        rows = pl.ds(pl.multiple_of(i * STEP, STEP), STEP)
        du = du_ref[rows, :]
        n = n_ref[rows, :]
        sums[0:1, :] += jnp.sum(du * n, axis=0, keepdims=True)
        sums[1:2, :] += jnp.sum(du, axis=0, keepdims=True)
        e = du * gain[...]
        e_mean = jnp.mean(e, axis=-1, keepdims=True)
        en_mean = jnp.mean(e * n, axis=-1, keepdims=True)
        dh_ref[rows, :] = (inv_ref[rows, 0:1] * (e - e_mean - n * en_mean)).astype(BF)
        return carry

    lax.fori_loop(0, ROWS // STEP, denormalise, 0)
    small[2 * half + 1 : 2 * half + 3, :] = sums[0:2, :]

    def lin_grad(i, carry):
        cols = pl.ds(pl.multiple_of(i * 256, 256), 256)
        g_lin[:, cols] = mm_tn(a3[...], dh_ref[:, cols])
        return carry

    lax.fori_loop(0, width // 256, lin_grad, 0)

    def later(v):
        return pltpu.roll(v.astype(F32), ROWS - 1, 0)

    ez3 = through_silu(mm_nt(dh_ref[...], lin[...]), z3[...])
    three[256:, :] = mm_tn(a2[...], ez3)
    three[:256, :] = mm_tn(a2[:, 256:], later(ez3).astype(BF))
    first = through_silu(mm_nt(ez3, w_three[256:512, :]), z2[:, :256])
    over = later(mm_nt(ez3, w_three[:256, :]))
    second = through_silu(mm_nt(ez3, w_three[512:, :]) + over, z2[:, 256:])
    side = mm_tn(a1[:, 256:], second)
    two[:256, :] = mm_tn(a1[:, 768:], later(first).astype(BF)) + side[:256]
    two[256:, :] = mm_tn(a1[:, :512], first) + side[256:]
    da = (
        mm_nt(first, w_two[256:512, :]),
        mm_nt(first, w_two[512:, :]) + mm_nt(second, w_two[:256, :]),
        mm_nt(second, w_two[256:512, :]),
        mm_nt(second, w_two[512:, :]) + later(mm_nt(first, w_two[:256, :])),
    )
    tops = (0, 80, 112, 16)
    total = None
    for j in (1, 2, 3):
        low, high = windows[j]
        ez = through_silu(da[j], z1[:, 256 * j : 256 * j + 256])
        term = mm_tn(xw[:, low:high], ez)[tops[j] : tops[j] + 240]
        total = term if total is None else total + term
    ez = through_silu(da[0], z1[:, :256])
    here = mm_tn(xw[:, :256], ez)[:160]
    gone = mm_tn(xw[:, 640:768], ez)[48:]
    one[...] = total + jnp.concatenate([gone, here], axis=0)
    for copy in started:
        copy.wait_send()


def step_kernel(tm_n, half, block_rows, scale, nz, work_count, *refs):
    ins, result, grads = refs[:11], refs[11], refs[12:17]
    work_refs, sum_refs = refs[17 : 17 + work_count], refs[17 + work_count :]
    work_kernel(tm_n, half, block_rows, scale, nz, *ins, *grads, *work_refs)
    sum_kernel(nz, tm_n // CORES, *grads, result, *sum_refs)


def work(operands, tm_n, half, block_rows, scale, nz):
    proj, lin = operands[3], operands[7]
    width = lin.shape[1]
    vmem = pl.BlockSpec(memory_space=pltpu.VMEM)
    ny = tm_n // CORES
    copies = 3 + (ny - 1) * (3 + (NX - 1) + 1 + 3 + (NX - 1) + 1)

    def buf(*shape, dtype=BF):
        return pltpu.VMEM(shape, dtype)

    shapes = ((240, 256), (768, 256), (768, 256), (256, width), (16, width))
    scratch = [
        buf(tm_n, *proj.shape),
        buf(768, 1024),
        buf(ROWS, 768),
        buf(RIM, 640),
        buf(RIM, 640),
        buf(RIM, 640),
        buf(ROWS, 1024, dtype=F32),
        buf(ROWS, 512, dtype=F32),
        buf(ROWS, 256, dtype=F32),
        buf(ROWS, 1024),
        buf(ROWS, 512),
        buf(ROWS, 256),
        buf(ROWS, width, dtype=F32),
        buf(ROWS, 128, dtype=F32),
        buf(ROWS, width),
        buf(ROWS, width, dtype=F32),
        buf(ROWS, width),
        buf(ROWS, width, dtype=F32),
        buf(tm_n, ROWS, 256),
        buf(ROWS, width),
        buf(8, width, dtype=F32),
        pltpu.SemaphoreType.DMA,
        pltpu.SemaphoreType.DMA((copies,)),
        pltpu.SemaphoreType.DMA((copies,)),
    ]
    grads = [buf(*shape, dtype=F32) for shape in shapes]
    packed = pl.pallas_call(
        functools.partial(step_kernel, tm_n, half, block_rows, scale, nz, len(scratch)),
        out_shape=jax.ShapeDtypeStruct((2 * CORES * NX * NX * PIECE, LANES), BF),
        in_specs=[pl.BlockSpec(memory_space=pltpu.SMEM)] + [vmem] * 10,
        out_specs=vmem,
        scratch_shapes=grads + scratch + sum_scratch(nz),
        compiler_params=pltpu.CompilerParams(
            collective_id=0, has_side_effects=True, vmem_limit_bytes=56 * 1024 * 1024
        ),
    )(*operands)
    return pl.pallas_call(
        unpack_kernel,
        out_shape=[jax.ShapeDtypeStruct(shape, BF) for shape in shapes],
        in_specs=[vmem],
        out_specs=[vmem] * len(shapes),
    )(packed)


def per_device(
    mel,
    cotangent,
    conv_one,
    conv_two,
    conv_three,
    linear_weight,
    ln_gain,
    ln_bias,
    proj,
    dw_kernel,
    blocks,
):
    tm_count = lax.axis_size("tm")
    dp_count = lax.axis_size("dp")
    block_rows = mel.shape[1] // dp_count
    taps = dw_kernel.shape[0]
    total_rows = (dp_count * dp_count + 2) // 3 * block_rows * tm_count
    one, two, three, lin, small = work(
        (
            blocks,
            mel,
            cotangent,
            proj,
            conv_one,
            conv_two,
            conv_three,
            linear_weight,
            ln_gain[None],
            ln_bias[None],
            dw_kernel,
        ),
        tm_count,
        taps // 2,
        block_rows,
        total_rows**-0.5,
        dp_count // NX,
    )
    return (one, two, three, lin, small[taps], small[taps + 1], small[:taps])


def solution(mesh):
    return jax.shard_map(
        per_device,
        mesh=mesh,
        in_specs=(
            P("dp", "tm", None),
            P("dp", "tm", None),
            P(),
            P(),
            P(),
            P(),
            P(),
            P(),
            P(None, "tm"),
            P(),
            P(),
        ),
        out_specs=(P(), P(), P(), P(), P(), P(), P()),
        check_vma=False,
    )
```
